128 devices in a mesh: row: 8 (over x_hi, z), rep: 16 (over x_lo, y, core).
Axes of the slice: x: 4 (x_hi: 2, x_lo: 2; x = x_hi * 2 + x_lo), y: 4, z: 4, core: 2. Of those that a mesh axis runs over, the one named last changes fastest.
Arguments:
- features: bfloat16 [32768, 256], P('row'), may hold values from 0 to 2
- self_weight: bfloat16 [256, 256], replicated, may hold values from -0.375 to 0.375
- neigh_weight: bfloat16 [256, 256], replicated, may hold values from -0.375 to 0.375
- out_bias: float32 [256], replicated, may hold values from -4 to 4
- tile_masks: int32 [32768, 128, 128], P('row', 'rep'), may hold values 0 or 1
- tile_live: int32 [256, 128], P('row', 'rep'), may hold values from 0 to 1, as said below
- tile_columns: int32 [256, 128], P('row', 'rep'), may hold values from 0 to 1
- node_degree: int32 [32768], P(('row', 'rep')), may hold values from 128 to 511
- cotangent: bfloat16 [32768, 256], P(('row', 'rep')), may hold values from -6 to 6
Outputs:
- hidden_out: bfloat16 [32768, 256], P(('row', 'rep'))
- grad_features: bfloat16 [32768, 256], P(('row', 'rep'))
- grad_self: float32 [256, 256], replicated
- grad_neigh: float32 [256, 256], replicated
- grad_bias: float32 [256], replicated
The draws below stay inside these ranges and needn't reach their ends.
Inputs may be any that keep to these rules, and one draw needn't show every extreme that they name: `tile_masks`: an edge bit; bits of slots without a tile are not read. `tile_live`: 1 where the slot holds a tile. `tile_columns`: the covered block among the 2 blocks of that column set and panel.
All inputs are finite; a program needn't handle non-finite values. No bound on the sum of `tile_masks` on one device may be relied on, other than what follows from the above.
Results may differ from the reference program's by a relative error of at most 0.0053.
Values may be sent and summed in bfloat16 or wider, within the bound.
A program may use at most 128 MiB of HBM per device.

```python
import math
import jax
import jax.numpy as jnp
from jax import lax

F = 256
TILE = 128
RBD = 2
PB = 32
PANEL = 4096
NODES = 32768
BLOCKS = 256
N_ROW = 8
N_REP = 16


def draw_tile_live(key, part):
    heavy_key, slot_key = jax.random.split(key)
    heavy = jax.random.randint(heavy_key, (N_ROW, 1, N_REP, 1), 0, 8) == 0
    rolls = jax.random.randint(slot_key, (N_ROW, PB, N_REP, N_ROW), 0, 20)
    limit = jnp.where(heavy, 18, 6)
    present = jnp.where(rolls < limit, 1, 0).astype(jnp.int32)
    return present.reshape(BLOCKS, N_REP * N_ROW)


def plant(values, key, low, high):
    extent = values.shape
    index_at = [jax.random.randint(jax.random.fold_in(key, axis), (), 0, extent[axis]) for axis in range(len(extent))]
    values = values.at[tuple(index_at)].set(low)
    longest = extent.index(max(extent))
    index_at[longest] = (index_at[longest] + 1) % extent[longest]
    return values.at[tuple(index_at)].set(high)


def block_scale(own_key, extent, cuts, smallest, high):
    gain, own = 1.0, jax.random.fold_in(own_key, 6)
    for dim, blocks in cuts:
        draws = jnp.exp(jax.random.uniform(jax.random.fold_in(own, dim), (blocks,), jnp.float32, smallest / len(cuts), high / len(cuts)))
        gain = gain * jnp.repeat(draws, extent[dim] // blocks).reshape([-1 if axis == dim else 1 for axis in range(len(extent))])
    return gain


def scatter_about(rng, extent, scale, bound, pieces=(), kind=jnp.bfloat16):
    factor_of = block_scale(rng, extent, pieces, -0.22, 0.18) if pieces else 1.0
    entries = jax.random.normal(rng, extent, jnp.float32) * scale * factor_of
    return jnp.minimum(jnp.maximum(entries, -bound), bound).astype(kind)


def setup_inputs(seed: int = 0) -> dict:
    streams_of = jax.random.split(jax.random.key(seed), 10)
    features = jnp.clip(2.0 * jax.random.uniform(streams_of[0], (NODES, F), jnp.float32) ** block_scale(streams_of[0], (NODES, F), ((0, 8),), -0.2, 0.2), 0.0, 2.0).astype(jnp.bfloat16)
    self_weight = scatter_about(streams_of[1], (F, F), F ** -0.5, 0.375)
    neigh_weight = scatter_about(streams_of[2], (F, F), F ** -0.5, 0.375)
    out_bias = scatter_about(streams_of[3], (F,), 1.0, 4.0, (), jnp.float32)
    tile_masks = plant((jax.random.randint(streams_of[4], (NODES, N_REP * N_ROW, TILE), 0, 32) < 1).astype(jnp.int32), jax.random.fold_in(streams_of[4], 1), 0, 1)
    tile_live = draw_tile_live(jax.random.fold_in(streams_of[9], 71), 0)
    tile_columns = plant(jax.random.randint(streams_of[6], (BLOCKS, N_REP * N_ROW), 0, RBD), jax.random.fold_in(streams_of[6], 1), 0, RBD - 1).astype(jnp.int32)
    node_degree = plant(jax.random.randint(streams_of[7], (NODES,), N_REP * N_ROW * TILE // 128, N_REP * N_ROW * TILE // 32), jax.random.fold_in(streams_of[7], 1), N_REP * N_ROW * TILE // 128, (N_REP * N_ROW * TILE // 32) - 1).astype(jnp.int32)
    cotangent = scatter_about(streams_of[8], (NODES, F), 1.0, 6.0, ((0, 128),))
    return dict(features=features, self_weight=self_weight, neigh_weight=neigh_weight, out_bias=out_bias, tile_masks=tile_masks, tile_live=tile_live, tile_columns=tile_columns, node_degree=node_degree, cotangent=cotangent)


def activation(values):
    return jax.nn.gelu(values, approximate=True)

def reference(features, self_weight, neigh_weight, out_bias, tile_masks, tile_live, tile_columns, node_degree, cotangent):
    highest = lax.Precision.HIGHEST
    column_sets = jnp.moveaxis(features.reshape(N_ROW, N_REP, RBD, TILE, F), 1, 0)
    masks = tile_masks.reshape(N_ROW, PB, TILE, N_REP, N_ROW, TILE)
    present = tile_live.reshape(N_ROW, PB, N_REP, N_ROW)
    chosen = tile_columns.reshape(N_ROW, PB, N_REP, N_ROW)
    degree = node_degree.reshape(N_ROW, PANEL, 1).astype(jnp.float32)
    panels = features.reshape(N_ROW, PANEL, F)
    cot_panels = cotangent.reshape(N_ROW, PANEL, F)
    scale = 1.0 / math.sqrt(NODES)
    panel_ids = jnp.arange(N_ROW).astype(jnp.int32)
    block_ids = jnp.arange(RBD).astype(jnp.int32)
    contract = (((0,), (0,)), ((), ()))
    outputs = []
    direct_rows = []
    grad_self = jnp.zeros((F, F), jnp.float32)
    grad_neigh = jnp.zeros((F, F), jnp.float32)
    grad_bias = jnp.zeros((F,), jnp.float32)
    transposed = jnp.zeros((N_ROW, N_REP, RBD, TILE, F), jnp.float32)
    for owner in range(N_ROW):
        set_masks = jnp.moveaxis(masks[owner], 2, 0)
        set_present = jnp.moveaxis(present[owner], 1, 0)
        set_chosen = jnp.moveaxis(chosen[owner], 1, 0)

        def forward_set(carry, inputs):
            mask_set, live_set, chosen_set, feature_set = inputs
            weights = mask_set.astype(jnp.float32) * live_set.astype(jnp.float32)[:, None, :, None]
            picked = feature_set[panel_ids[None, :], chosen_set].astype(jnp.float32)
            return (carry + jnp.einsum('pisj,psjf->pif', weights, picked, precision=highest), None)
        agg_sum, _ = lax.scan(forward_set, jnp.zeros((PB, TILE, F), jnp.float32), (set_masks, set_present, set_chosen, column_sets))
        agg_sum = agg_sum.reshape(PANEL, F)
        mean = (agg_sum / degree[owner]).astype(jnp.bfloat16)
        own = panels[owner]
        pre = jnp.dot(own, self_weight, preferred_element_type=jnp.float32) + jnp.dot(mean, neigh_weight, preferred_element_type=jnp.float32) + out_bias.astype(jnp.float32)
        result, pull = jax.vjp(activation, pre)
        outputs.append(result.astype(jnp.bfloat16))
        dpre = pull(cot_panels[owner].astype(jnp.float32))[0]
        dpre_b = dpre.astype(jnp.bfloat16)
        grad_self = grad_self + lax.dot_general(own, dpre_b, contract, preferred_element_type=jnp.float32)
        grad_neigh = grad_neigh + lax.dot_general(mean, dpre_b, contract, preferred_element_type=jnp.float32)
        grad_bias = grad_bias + lax.optimization_barrier(jnp.sum(dpre, axis=0))
        message = (jnp.dot(dpre_b, neigh_weight.T, preferred_element_type=jnp.float32) / degree[owner]).astype(jnp.bfloat16)
        direct_rows.append(jnp.dot(dpre_b, self_weight.T, preferred_element_type=jnp.float32))
        message_blocks = message.reshape(PB, TILE, F).astype(jnp.float32)

        def backward_set(inputs):
            mask_set, live_set, chosen_set = inputs
            weights = mask_set.astype(jnp.float32) * live_set.astype(jnp.float32)[:, None, :, None]
            per_tile = jnp.einsum('pisj,pif->psjf', weights, message_blocks, precision=highest)
            onehot = (chosen_set[:, :, None] == block_ids[None, None, :]).astype(jnp.float32)
            return jnp.einsum('psb,psjf->sbjf', onehot, per_tile, precision=highest)
        spread = lax.map(backward_set, (set_masks, set_present, set_chosen))
        transposed = transposed + jnp.moveaxis(spread, 0, 1)
    hidden_out = jnp.stack(outputs).reshape(NODES, F)
    direct = jnp.stack(direct_rows)
    grad_features = (direct + transposed.reshape(N_ROW, PANEL, F)).astype(jnp.bfloat16).reshape(NODES, F)
    return (hidden_out, grad_features, grad_self * scale, grad_neigh * scale, grad_bias * scale)
```

```python
import functools
import math

import jax
import jax.numpy as jnp
from jax import lax
from jax.experimental import pallas as pl
from jax.experimental.pallas import tpu as pltpu
from jax.sharding import PartitionSpec as P

BF = jnp.bfloat16
F32 = jnp.float32
BUFFERS = 4
CONTRACT_LAST = (((1,), (1,)), ((), ()))
CONTRACT_FIRST = (((0,), (0,)), ((), ()))


def kernel(
    rows_n,
    reps_n,
    scale,
    features,
    self_weight,
    neigh_weight,
    bias,
    masks,
    live,
    column,
    degree,
    cotangent,
    hidden_out,
    grad_features,
    grad_self,
    grad_neigh,
    grad_bias,
    dense,
    mask_buf,
    gathered,
    sw_v,
    nw_v,
    bias_v,
    degree_v,
    cot_v,
    own_acc,
    pair_send,
    pair_recv,
    part_send,
    part_recv,
    agg,
    msg,
    msg_recv,
    msg_sib,
    back,
    direct,
    back_send,
    back_recv,
    g1_send,
    g1_recv,
    g1_sum,
    g2_send,
    g2_recv,
    g3,
    g4,
    hid_v,
    gf_v,
    gs_v,
    gn_v,
    gb_v,
    mask_sem,
    in_sem,
    out_sem,
    s1,
    r1,
    s2p,
    r2p,
    s2,
    r2,
    s3,
    r3,
    s3f,
    r3f,
    s4,
    r4,
    sg1,
    rg1,
    sg2,
    rg2,
    sg3,
    rg3,
    sg4,
    rg4,
):
    width = self_weight.shape[0]
    share = cotangent.shape[0]
    tile = masks.shape[1]
    half_rows = rows_n // 2
    chips = reps_n // 2
    mask_rows = tile * rows_n
    blocks = masks.shape[0] // mask_rows
    slot_width = share
    row = lax.axis_index("row")
    rep = lax.axis_index("rep")
    core = rep % 2
    chip = rep // 2
    sibling = chip * 2 + 1 - core
    far_rep = (rep + reps_n // 2) % reps_n

    def remote(src, dst, send, recv, to_row, to_rep):
        return pltpu.make_async_remote_copy(
            src_ref=src,
            dst_ref=dst,
            send_sem=send,
            recv_sem=recv,
            device_id=(to_row, to_rep),
            device_id_type=pl.DeviceIdType.MESH,
        )

    def mask_copy(block, slot):
        return pltpu.make_async_copy(
            masks.at[pl.ds(block * mask_rows, mask_rows), :], mask_buf.at[slot], mask_sem.at[slot]
        )

    for block in range(BUFFERS):
        mask_copy(block, block).start()
    inputs = [
        pltpu.make_async_copy(src, dst, in_sem.at[index])
        for index, (src, dst) in enumerate(
            (
                (self_weight, sw_v),
                (neigh_weight, nw_v),
                (bias, bias_v),
                (degree, degree_v),
                (cotangent, cot_v),
                (
                    features.at[pl.ds(rep * share, share), :],
                    gathered.at[pl.ds(row * share, share), :],
                ),
            )
        )
    ]

    def row_at(far, step):
        return ((row // half_rows + far) % 2) * half_rows + (row % half_rows + step) % half_rows

    row_steps = [
        (far, step) for step in range(half_rows) for far in range(2) if (far, step) != (0, 0)
    ]

    def greet(to_row, to_rep):
        pl.semaphore_signal(
            barrier, inc=1, device_id=(to_row, to_rep), device_id_type=pl.DeviceIdType.MESH
        )

    barrier = pltpu.get_barrier_semaphore()
    greeted = 0
    for step in range(1, reps_n):
        greet(row, (rep + step) % reps_n)
        greeted += 1
    for far, step in row_steps:
        greet(row_at(far, step), rep)
        greeted += 1
        if far:
            greet(row_at(far, step), far_rep)
            greeted += 1
    pl.semaphore_wait(barrier, greeted)

    def feature_copy(far, step):
        to_rep = far_rep if far else rep
        return remote(
            features.at[pl.ds(to_rep * share, share), :],
            gathered.at[pl.ds(row * share, share), :],
            s1.at[far * half_rows + step],
            r1.at[far * half_rows + step],
            row_at(far, step),
            to_rep,
        )

    for far, step in row_steps:
        feature_copy(far, step).start()
    for copy in inputs:
        copy.start()

    def expand(block, carry):
        slot = block % BUFFERS
        mask_copy(block, slot).wait()
        at = pl.ds(pl.multiple_of(block * tile, tile), tile)
        for s in range(rows_n):
            bits = mask_buf[slot, pl.ds(s, tile, stride=rows_n), :].astype(F32)
            held = live[s, block].astype(F32)
            second = held * column[s, block].astype(F32)
            first = held - second
            dense[at, s * slot_width : s * slot_width + tile] = (bits * first).astype(BF)
            dense[at, s * slot_width + tile : (s + 1) * slot_width] = (bits * second).astype(BF)

        @pl.when(block + BUFFERS < blocks)
        def _():
            mask_copy(block + BUFFERS, slot).start()

        return carry

    lax.fori_loop(0, blocks, expand, 0)
    for copy in inputs:
        copy.wait()
    for far, step in row_steps:
        feature_copy(far, step).wait_recv()

    def share_rows(index):
        return pl.ds(pl.multiple_of(index * share, share), share)

    def pair_copy(t):
        return remote(pair_send.at[t], pair_recv.at[t], s2p.at[t], r2p.at[t], row, sibling)

    def part_copy(t):
        return remote(
            part_send.at[t],
            part_recv.at[t],
            s2.at[t],
            r2.at[t],
            row,
            ((chip + 1 + t) % chips) * 2 + core,
        )

    def finish_pair(t):
        pair_copy(t).wait_recv()
        part_send[t] = (own_acc[t % 2] + pair_recv[t].astype(F32)).astype(BF)
        part_copy(t).start()

    def forward(t, carry):
        at = (chip + 1 + t) % chips
        pair_send[t] = jnp.dot(
            dense[share_rows(at * 2 + 1 - core), :], gathered[...], preferred_element_type=F32
        ).astype(BF)
        pair_copy(t).start()

        own_acc[t % 2] = jnp.dot(
            dense[share_rows(at * 2 + core), :], gathered[...], preferred_element_type=F32
        )

        @pl.when(t > 0)
        def _():
            finish_pair(t - 1)

        return carry

    lax.fori_loop(0, chips, forward, 0)
    pair_copy(chips - 1).wait_recv()
    agg[...] = own_acc[(chips - 1) % 2] + pair_recv[chips - 1].astype(F32)
    own = gathered[share_rows(row), :]
    pre_own = jnp.dot(own, sw_v[...], preferred_element_type=F32) + bias_v[...]
    direct[...] = pre_own
    degree_row = degree_v[...].astype(F32)
    degree_column = jnp.transpose(jnp.broadcast_to(degree_row, (width, share)))
    for t in range(chips - 1):
        part_copy(t).wait_recv()
        agg[...] += part_recv[t].astype(F32)

    mean = (agg[...] / degree_column).astype(BF)
    pre = direct[...] + jnp.dot(mean, nw_v[...], preferred_element_type=F32)
    root = math.sqrt(2.0 / math.pi)
    square = pre * pre
    bend = jnp.tanh(root * (pre + 0.044715 * (square * pre)))
    hid_v[...] = (0.5 * pre * (1.0 + bend)).astype(BF)
    slope = 0.5 * (1.0 + bend) + (0.5 * root) * pre * (1.0 - bend * bend) * (
        1.0 + (3.0 * 0.044715) * square
    )
    dpre = cot_v[...].astype(F32) * slope
    dpre_b = dpre.astype(BF)
    msg[...] = (
        lax.dot_general(nw_v[...], dpre_b, CONTRACT_LAST, preferred_element_type=F32) / degree_row
    ).astype(BF)

    def msg_copy(t):
        return remote(
            msg, msg_recv.at[t], s3.at[t], r3.at[t], row, ((chip + 1 + t) % chips) * 2 + core
        )

    def sib_copy(src, t):
        return remote(src, msg_sib.at[t], s3f.at[t], r3f.at[t], row, sibling)

    sib_copy(msg, chips - 1).start()
    for t in range(chips - 1):
        msg_copy(t).start()

    outs = [
        pltpu.make_async_copy(src, dst, out_sem.at[index])
        for index, (src, dst) in enumerate(
            (
                (hid_v, hidden_out),
                (gs_v, grad_self),
                (gn_v, grad_neigh),
                (gb_v, grad_bias),
                (gf_v, grad_features),
            )
        )
    ]
    outs[0].start()

    g_rows = 2 * width // rows_n
    lanes = width // 2
    tile_rows = g_rows // (reps_n // 2)
    terms = [
        lax.dot_general(left, dpre_b, CONTRACT_FIRST, preferred_element_type=F32) * scale
        for left in (own, mean)
    ]
    bias_term = jnp.sum(dpre, axis=0, keepdims=True) * scale
    for index in range(rows_n):
        term = terms[index * g_rows // width]
        low = index * g_rows % width
        for side in range(2):
            g1_send[index, side * (reps_n // 2) : (side + 1) * (reps_n // 2)] = term[
                low : low + g_rows, side * lanes : (side + 1) * lanes
            ].reshape(reps_n // 2, tile_rows, lanes)
        for side in range(2):
            g1_send[index, reps_n + side] = jnp.broadcast_to(
                bias_term[:, side * lanes : (side + 1) * lanes], (tile_rows, lanes)
            )

    def g1_copy(far, step):
        index = far * half_rows + step
        to_row = row_at(far, step)
        return remote(
            g1_send.at[to_row], g1_recv.at[index], sg1.at[index], rg1.at[index], to_row, rep
        )

    for far, step in row_steps:
        g1_copy(far, step).start()
    direct[...] = lax.dot_general(sw_v[...], dpre_b, CONTRACT_LAST, preferred_element_type=F32)

    def spread(block, owner, start):
        at = share_rows(owner)
        for s in range(rows_n):
            term = jnp.dot(
                block, dense[at, s * slot_width : (s + 1) * slot_width], preferred_element_type=F32
            )
            if start:
                back[s] = term
            else:
                back[s] += term

    def backward(t, carry):
        source = (chip + chips - 1 - t) % chips
        msg_copy(t).wait_recv()
        sib_copy(msg_recv.at[t], t).start()
        spread(msg_recv[t], source * 2 + core, False)
        sib_copy(msg_recv.at[t], t).wait_recv()
        spread(msg_sib[t], source * 2 + 1 - core, False)
        return carry

    spread(msg[...], rep, True)
    sib_copy(msg, chips - 1).wait_recv()
    spread(msg_sib[chips - 1], sibling, False)
    lax.fori_loop(0, chips - 1, backward, 0)

    def back_copy(far, step):
        index = far * half_rows + step
        return remote(
            back_send.at[index],
            back_recv.at[index],
            s4.at[index],
            r4.at[index],
            row_at(far, step),
            rep,
        )

    for far, step in row_steps:
        back_send[far * half_rows + step] = back[row_at(far, step)].astype(BF)
        back_copy(far, step).start()

    total = g1_send[row]
    for far, step in row_steps:
        g1_copy(far, step).wait_recv()
        total = total + g1_recv[far * half_rows + step]
    g1_sum[...] = total
    for index in range(reps_n):
        g2_send[index, 0] = g1_sum[index]
        g2_send[index, 1] = g1_sum[reps_n]
        g2_send[index, 2] = g1_sum[reps_n + 1]

    def g2_copy(step):
        to_rep = (rep + step) % reps_n
        return remote(g2_send.at[to_rep], g2_recv.at[step], sg2.at[step], rg2.at[step], row, to_rep)

    for step in range(1, reps_n):
        g2_copy(step).start()
    total = g2_send[rep]
    for step in range(1, reps_n):
        g2_copy(step).wait_recv()
        total = total + g2_recv[step]
    g3[row] = total[0]
    for side in range(2):
        gb_v[:, side * lanes : (side + 1) * lanes] = total[1 + side][0:1, :]
    outs[3].start()

    def g3_copy(far, step):
        index = far * half_rows + step
        return remote(
            g3.at[row], g3.at[row], sg3.at[index], rg3.at[index], row_at(far, step), rep
        )

    for far, step in row_steps:
        g3_copy(far, step).start()
    for far, step in row_steps:
        g3_copy(far, step).wait_recv()

    def g4_copy(step):
        return remote(
            g3, g4.at[rep], sg4.at[step], rg4.at[step], row, (rep + step) % reps_n
        )

    for step in range(1, reps_n):
        g4_copy(step).start()
    g4[rep] = g3[...]
    for step in range(1, reps_n):
        g4_copy(step).wait_recv()
    for index in range(rows_n):
        out = (gs_v, gn_v)[index * g_rows // width]
        low = index * g_rows % width
        for side in range(2):
            out[low : low + g_rows, side * lanes : (side + 1) * lanes] = g4[
                side * (reps_n // 2) : (side + 1) * (reps_n // 2), index
            ].reshape(g_rows, lanes)
    outs[1].start()
    outs[2].start()

    direct[...] += back[row]
    for far, step in row_steps:
        back_copy(far, step).wait_recv()
        direct[...] += back_recv[far * half_rows + step].astype(F32)
    gf_v[...] = jnp.transpose(direct[...]).astype(BF)
    outs[4].start()

    for far, step in row_steps:
        feature_copy(far, step).wait_send()
        g1_copy(far, step).wait_send()
        back_copy(far, step).wait_send()
        g3_copy(far, step).wait_send()
    for t in range(chips):
        pair_copy(t).wait_send()
    for t in range(chips - 1):
        part_copy(t).wait_send()
        msg_copy(t).wait_send()
        sib_copy(msg_recv.at[t], t).wait_send()
    sib_copy(msg, chips - 1).wait_send()
    for step in range(1, reps_n):
        g2_copy(step).wait_send()
        g4_copy(step).wait_send()
    for copy in outs:
        copy.wait()


def per_device(
    features,
    self_weight,
    neigh_weight,
    out_bias,
    tile_masks,
    tile_live,
    tile_columns,
    node_degree,
    cotangent,
):
    rows_n = lax.axis_size("row")
    reps_n = lax.axis_size("rep")
    panel_rows, width = features.shape
    share = node_degree.shape[0]
    slots = tile_masks.shape[1]
    tile = tile_masks.shape[2]
    chips = reps_n // 2
    lanes = width // 2
    tile_rows = 2 * width // rows_n // (reps_n // 2)
    scale = 1.0 / math.sqrt(share * rows_n * reps_n)
    block = (share, width)
    anywhere = pl.BlockSpec(memory_space=pl.ANY)
    scalars = pl.BlockSpec(memory_space=pltpu.SMEM)
    dma = pltpu.SemaphoreType.DMA
    vmem = pltpu.VMEM
    grads = (reps_n + 2, tile_rows, lanes)
    scratch = [
        vmem((panel_rows, slots * share), BF),
        vmem((BUFFERS, tile * slots, tile), jnp.int32),
        vmem((rows_n * share, width), BF),
        vmem((width, width), BF),
        vmem((width, width), BF),
        vmem((1, width), F32),
        vmem((1, share), jnp.int32),
        vmem(block, BF),
        vmem((2, *block), F32),
        vmem((chips, *block), BF),
        vmem((chips, *block), BF),
        vmem((chips, *block), BF),
        vmem((chips, *block), BF),
        vmem(block, F32),
        vmem((width, share), BF),
        vmem((chips, width, share), BF),
        vmem((chips, width, share), BF),
        vmem((rows_n, width, share), F32),
        vmem((width, share), F32),
        vmem((rows_n, width, share), BF),
        vmem((rows_n, width, share), BF),
        vmem((rows_n, *grads), F32),
        vmem((rows_n, *grads), F32),
        vmem(grads, F32),
        vmem((reps_n, 3, tile_rows, lanes), F32),
        vmem((reps_n, 3, tile_rows, lanes), F32),
        vmem((rows_n, tile_rows, lanes), F32),
        vmem((reps_n, rows_n, tile_rows, lanes), F32),
        vmem(block, BF),
        vmem(block, BF),
        vmem((width, width), F32),
        vmem((width, width), F32),
        vmem((1, width), F32),
        dma((BUFFERS,)),
        dma((6,)),
        dma((5,)),
        dma((rows_n,)),
        dma((rows_n,)),
        dma((chips,)),
        dma((chips,)),
        dma((chips,)),
        dma((chips,)),
        dma((chips,)),
        dma((chips,)),
        dma((chips,)),
        dma((chips,)),
        dma((rows_n,)),
        dma((rows_n,)),
        dma((rows_n,)),
        dma((rows_n,)),
        dma((reps_n,)),
        dma((reps_n,)),
        dma((rows_n,)),
        dma((rows_n,)),
        dma((reps_n,)),
        dma((reps_n,)),
    ]
    hidden, grad_features, grad_self, grad_neigh, grad_bias = pl.pallas_call(
        functools.partial(kernel, rows_n, reps_n, scale),
        out_shape=(
            jax.ShapeDtypeStruct(block, BF),
            jax.ShapeDtypeStruct(block, BF),
            jax.ShapeDtypeStruct((width, width), F32),
            jax.ShapeDtypeStruct((width, width), F32),
            jax.ShapeDtypeStruct((1, width), F32),
        ),
        in_specs=[anywhere] * 5 + [scalars] * 2 + [anywhere] * 2,
        out_specs=(anywhere,) * 5,
        scratch_shapes=scratch,
        compiler_params=pltpu.CompilerParams(
            collective_id=0, has_side_effects=True, vmem_limit_bytes=56 * 1024 * 1024
        ),
        name="layer",
    )(
        features,
        self_weight,
        neigh_weight,
        out_bias.reshape(1, width),
        tile_masks.reshape(panel_rows * slots, tile),
        tile_live.T,
        tile_columns.T,
        node_degree.reshape(1, share),
        cotangent,
    )
    return (hidden, grad_features, grad_self, grad_neigh, grad_bias.reshape(width))


def solution(mesh):
    return jax.shard_map(
        per_device,
        mesh=mesh,
        in_specs=(
            P("row", None),
            P(),
            P(),
            P(),
            P("row", "rep", None),
            P("row", "rep"),
            P("row", "rep"),
            P(("row", "rep")),
            P(("row", "rep"), None),
        ),
        out_specs=(P(("row", "rep"), None), P(("row", "rep"), None), P(), P(), P()),
        check_vma=False,
    )
```

```python
import functools
import math

import jax
import jax.numpy as jnp
from jax import lax
from jax.experimental import pallas as pl
from jax.experimental.pallas import tpu as pltpu
from jax.sharding import PartitionSpec as P

BF = jnp.bfloat16
F32 = jnp.float32
BUFFERS = 16
CONTRACT_LAST = (((1,), (1,)), ((), ()))
CONTRACT_FIRST = (((0,), (0,)), ((), ()))


def kernel(
    rows_n,
    reps_n,
    scale,
    features,
    self_weight,
    neigh_weight,
    bias,
    masks,
    live,
    column,
    degree,
    cotangent,
    hidden_out,
    grad_features,
    grad_self,
    grad_neigh,
    grad_bias,
    dense,
    mask_buf,
    feat_v,
    gathered,
    sw_v,
    nw_v,
    bias_v,
    degree_v,
    cot_v,
    work,
    pair_send,
    pair_recv,
    part_send,
    part_recv,
    own_sum,
    pre_v,
    mean_v,
    msg_all,
    direct,
    back_own,
    back_send,
    back_recv,
    g1_send,
    g1_recv,
    g1_sum,
    g2_send,
    g2_recv,
    g3,
    g4,
    hid_v,
    gf_v,
    gs_v,
    gn_v,
    gb_v,
    mask_sem,
    in_sem,
    out_sem,
    s1,
    r1,
    s2p,
    r2p,
    s2,
    r2,
    s3,
    r3,
    s3f,
    r3f,
    s4,
    r4,
    sg1,
    rg1,
    sg2,
    rg2,
    sg3,
    rg3,
    sg4,
    rg4,
    sg4f,
    rg4f,
):
    width = self_weight.shape[0]
    share = cotangent.shape[0]
    half = width // 2
    tile = masks.shape[1]
    half_rows = rows_n // 2
    chips = reps_n // 2
    ring = chips // 2
    mask_rows = tile * rows_n
    blocks = masks.shape[0] // mask_rows
    slot_width = share
    row = lax.axis_index("row")
    rep = lax.axis_index("rep")
    core = rep % 2
    chip = rep // 2
    sibling = chip * 2 + 1 - core
    far_rep = (rep + reps_n // 2) % reps_n

    def remote(src, dst, send, recv, to_row, to_rep):
        return pltpu.make_async_remote_copy(
            src_ref=src,
            dst_ref=dst,
            send_sem=send,
            recv_sem=recv,
            device_id=(to_row, to_rep),
            device_id_type=pl.DeviceIdType.MESH,
        )

    def share_rows(index):
        return pl.ds(pl.multiple_of(index * share, share), share)

    def row_at(far, step):
        return ((row // half_rows + far) % 2) * half_rows + (row % half_rows + step) % half_rows

    def chip_at(across, along):
        return ((chip // ring + across) % 2) * ring + (chip % ring + along) % ring

    def chip_from(across, along):
        return ((chip // ring + across) % 2) * ring + (chip % ring + ring - along) % ring

    def offset(t, size):
        across = (t + 1) % 2
        turn = t // 2
        return across, (across * (1 + turn) + (1 - across) * (size - 1 - turn)) % size

    row_steps = [
        (far, step) for step in range(half_rows) for far in range(2) if (far, step) != (0, 0)
    ]

    def mask_copy(block, slot):
        return pltpu.make_async_copy(
            masks.at[pl.ds(pl.multiple_of(block * mask_rows, mask_rows), mask_rows), :],
            mask_buf.at[slot],
            mask_sem.at[slot],
        )

    def greet(to_row, to_rep):
        pl.semaphore_signal(
            barrier, inc=1, device_id=(to_row, to_rep), device_id_type=pl.DeviceIdType.MESH
        )

    barrier = pltpu.get_barrier_semaphore()
    greeted = 0
    for far, step in row_steps:
        greet(row_at(far, step), rep)
        greeted += 1
        if far:
            greet(row_at(far, step), far_rep)
            greeted += 1
    for step in range(1, reps_n):
        greet(row, (rep + step) % reps_n)
        greeted += 1

    inputs = [
        pltpu.make_async_copy(src, dst, in_sem.at[index])
        for index, (src, dst) in enumerate(
            (
                (features.at[share_rows(rep), :], feat_v.at[0]),
                (features.at[share_rows(far_rep), :], feat_v.at[1]),
                (self_weight, sw_v),
                (neigh_weight, nw_v),
                (bias, bias_v),
                (degree, degree_v),
                (cotangent, cot_v),
            )
        )
    ]
    inputs[0].start()
    inputs[1].start()
    for block in range(BUFFERS):
        mask_copy(block, block).start()
    for copy in inputs[2:]:
        copy.start()

    def expand(block, carry):
        slot = block % BUFFERS
        mask_copy(block, slot).wait()
        at = pl.ds(pl.multiple_of(block * tile, tile), tile)
        for s in range(rows_n):
            bits = mask_buf[slot, pl.ds(s, tile, stride=rows_n), :].astype(F32)
            held = live[s, block].astype(F32)
            second = held * column[s, block].astype(F32)
            first = held - second
            dense[at, s * slot_width : s * slot_width + tile] = (bits * first).astype(BF)
            dense[at, s * slot_width + tile : (s + 1) * slot_width] = (bits * second).astype(BF)

        @pl.when(block + BUFFERS < blocks)
        def _():
            mask_copy(block + BUFFERS, slot).start()

        return carry

    def feature_copy(part, far, step):
        return remote(
            feat_v.at[far, :, part * half : (part + 1) * half],
            gathered.at[part, share_rows(row), :],
            s1.at[part, far * half_rows + step],
            r1.at[part, far * half_rows + step],
            row_at(far, step),
            far_rep if far else rep,
        )

    lax.fori_loop(0, blocks // 2, expand, 0)
    inputs[0].wait()
    inputs[1].wait()
    pl.semaphore_wait(barrier, greeted)
    for far, step in row_steps:
        feature_copy(0, far, step).start()
    lax.fori_loop(blocks // 2, blocks, expand, 0)
    for copy in inputs[2:]:
        copy.wait()
    for part in range(2):
        gathered[part, share_rows(row), :] = feat_v[0, :, part * half : (part + 1) * half]
    own = feat_v[0]
    pre_v[...] = jnp.dot(own, sw_v[...], preferred_element_type=F32) + bias_v[...]
    degree_row = degree_v[...].astype(F32)
    degree_column = jnp.transpose(jnp.broadcast_to(degree_row, (half, share)))
    for far, step in row_steps:
        feature_copy(0, far, step).wait_send()
    for far, step in row_steps:
        feature_copy(1, far, step).start()

    def pair_copy(part, t):
        return remote(
            pair_send.at[part, t],
            pair_recv.at[part, t],
            s2p.at[part, t],
            r2p.at[part, t],
            row,
            sibling,
        )

    def part_copy(part, t):
        return remote(
            part_send.at[part, t],
            part_recv.at[part, t],
            s2.at[part, t],
            r2.at[part, t],
            row,
            chip_at(*offset(t, ring)) * 2 + core,
        )

    def finish_pair(part, t):
        pair_copy(part, t).wait_recv()
        part_send[part, t] = (work[t % 2, core] + pair_recv[part, t].astype(F32)).astype(BF)
        part_copy(part, t).start()

    def forward(part):
        def body(t, carry):
            at = chip_at(*offset(t, ring))
            rows = pl.ds(pl.multiple_of(at * (2 * share), 2 * share), 2 * share)
            work[t % 2] = jnp.dot(
                dense[rows, :], gathered[part], preferred_element_type=F32
            ).reshape(2, share, half)
            pair_send[part, t] = work[t % 2, 1 - core].astype(BF)
            pair_copy(part, t).start()

            @pl.when(t > 0)
            def _():
                finish_pair(part, t - 1)

            return carry

        for far, step in row_steps:
            feature_copy(part, far, step).wait_recv()
        lax.fori_loop(0, chips, body, 0)
        pair_copy(part, chips - 1).wait_recv()
        own_sum[part] = work[(chips - 1) % 2, core] + pair_recv[part, chips - 1].astype(F32)

    forward(0)
    forward(1)
    for part in range(2):
        total = own_sum[part]
        for t in range(chips - 1):
            part_copy(part, t).wait_recv()
            total = total + part_recv[part, t].astype(F32)
        mean = (total / degree_column).astype(BF)
        mean_v[:, part * half : (part + 1) * half] = mean
        pre_v[...] += jnp.dot(
            mean, nw_v[part * half : (part + 1) * half, :], preferred_element_type=F32
        )

    pre = pre_v[...]
    root = math.sqrt(2.0 / math.pi)
    square = pre * pre
    bend = jnp.tanh(root * (pre + 0.044715 * (square * pre)))
    slope = 0.5 * (1.0 + bend) + (0.5 * root) * pre * (1.0 - bend * bend) * (
        1.0 + (3.0 * 0.044715) * square
    )
    dpre = cot_v[...].astype(F32) * slope
    dpre_b = dpre.astype(BF)

    def message_copy(part, across, along):
        relay = across and along
        source = (chip_at(1, 0) if relay else chip) * 2 + core
        place = msg_all.at[part, :, share_rows(source)]
        index = across * ring + along
        target = chip_at(0 if relay else across, along) * 2 + core
        return remote(place, place, s3.at[part, index], r3.at[part, index], row, target)

    def sibling_copy(part, across, along):
        place = msg_all.at[part, :, share_rows(chip_from(across, along) * 2 + core)]
        index = across * ring + along
        return remote(place, place, s3f.at[part, index], r3f.at[part, index], row, sibling)

    along_order = sorted(range(1, ring), key=lambda d: min(d, ring - d))

    def send_messages(part):
        message_copy(part, 1, 0).start()
        for along in along_order:
            message_copy(part, 0, along).start()
        sibling_copy(part, 0, 0).start()

    def relay_messages(part):
        message_copy(part, 1, 0).wait_recv()
        for along in along_order:
            message_copy(part, 1, along).start()
        sibling_copy(part, 1, 0).start()

    def finish_messages(part):
        for across in range(2):
            for along in along_order:
                message_copy(part, across, along).wait_recv()
                sibling_copy(part, across, along).start()
        for across in range(2):
            for along in range(ring):
                sibling_copy(part, across, along).wait_recv()

    for part in range(2):
        msg_all[part, :, share_rows(rep)] = (
            lax.dot_general(
                nw_v[part * half : (part + 1) * half, :],
                dpre_b,
                CONTRACT_LAST,
                preferred_element_type=F32,
            )
            / degree_row
        ).astype(BF)
        if part == 0:
            send_messages(0)

    outs = [
        pltpu.make_async_copy(src, dst, out_sem.at[index])
        for index, (src, dst) in enumerate(
            (
                (hid_v, hidden_out),
                (gs_v, grad_self),
                (gn_v, grad_neigh),
                (gb_v, grad_bias),
                (gf_v, grad_features),
            )
        )
    ]
    hid_v[...] = (0.5 * pre * (1.0 + bend)).astype(BF)
    outs[0].start()

    g_rows = 2 * width // rows_n
    tile_rows = g_rows // (reps_n // 2)
    terms = [
        lax.dot_general(left, dpre_b, CONTRACT_FIRST, preferred_element_type=F32) * scale
        for left in (feat_v[0], mean_v[...])
    ]
    bias_term = jnp.sum(dpre, axis=0, keepdims=True) * scale
    for index in range(rows_n):
        term = terms[index * g_rows // width]
        low = index * g_rows % width
        for side in range(2):
            g1_send[index, side * (reps_n // 2) : (side + 1) * (reps_n // 2)] = term[
                low : low + g_rows, side * half : (side + 1) * half
            ].reshape(reps_n // 2, tile_rows, half)
            g1_send[index, reps_n + side] = jnp.broadcast_to(
                bias_term[:, side * half : (side + 1) * half], (tile_rows, half)
            )

    def g1_copy(far, step):
        index = far * half_rows + step
        to_row = row_at(far, step)
        return remote(
            g1_send.at[to_row],
            g1_recv.at[index],
            sg1.at[index],
            rg1.at[index],
            to_row,
            far_rep if far else rep,
        )

    for far, step in row_steps:
        g1_copy(far, step).start()
    direct[...] = lax.dot_general(
        sw_v[...], dpre_b, CONTRACT_LAST, preferred_element_type=F32
    ).reshape(2, half, share)

    def back_copy(part, t):
        return remote(
            back_send.at[part, t],
            back_recv.at[part, t],
            s4.at[part, t],
            r4.at[part, t],
            row_at(*offset(t, half_rows)),
            rep,
        )

    def backward(part):
        def body(t, carry):
            target = row_at(*offset(t, half_rows))
            columns = pl.ds(pl.multiple_of(target * slot_width, slot_width), slot_width)
            term = jnp.dot(msg_all[part], dense[:, columns], preferred_element_type=F32)

            @pl.when(t < rows_n - 1)
            def _():
                back_send[part, t] = term.astype(BF)
                back_copy(part, t).start()

            @pl.when(t == rows_n - 1)
            def _():
                back_own[part] = term

            return carry

        lax.fori_loop(0, rows_n, body, 0)

    relay_messages(0)
    finish_messages(0)
    send_messages(1)
    backward(0)

    def g2_copy(step):
        to_rep = (rep + step) % reps_n
        return remote(g2_send.at[to_rep], g2_recv.at[step], sg2.at[step], rg2.at[step], row, to_rep)

    def g3_copy(far, step):
        index = far * half_rows + step
        return remote(g3.at[row], g3.at[row], sg3.at[index], rg3.at[index], row_at(far, step), rep)

    def g4_copy(t):
        return remote(
            g3, g4.at[rep], sg4.at[t], rg4.at[t], row, chip_at(*offset(t, ring)) * 2 + core
        )

    def g4_pair(t):
        source = chip_from(*offset(t, ring)) * 2 + core
        return remote(g4.at[source], g4.at[source], sg4f.at[t], rg4f.at[t], row, sibling)

    relay_messages(1)
    total = g1_send[row]
    for far, step in row_steps:
        g1_copy(far, step).wait_recv()
        total = total + g1_recv[far * half_rows + step]
    g1_sum[...] = total
    for index in range(reps_n):
        g2_send[index, 0] = g1_sum[index]
        g2_send[index, 1] = g1_sum[reps_n]
        g2_send[index, 2] = g1_sum[reps_n + 1]
    for step in range(1, reps_n):
        g2_copy(step).start()

    finish_messages(1)
    backward(1)

    total = g2_send[rep]
    for step in range(1, reps_n):
        g2_copy(step).wait_recv()
        total = total + g2_recv[step]
    g3[row] = total[0]
    for far, step in row_steps:
        g3_copy(far, step).start()
    for side in range(2):
        gb_v[:, side * half : (side + 1) * half] = total[1 + side][0:1, :]
    outs[3].start()

    def column_sums(part):
        total = direct[part] + back_own[part]
        for t in range(rows_n - 1):
            back_copy(part, t).wait_recv()
            total = total + back_recv[part, t].astype(F32)
        gf_v[:, part * half : (part + 1) * half] = jnp.transpose(total).astype(BF)

    column_sums(0)
    for far, step in row_steps:
        g3_copy(far, step).wait_recv()
    for t in range(chips - 1):
        g4_copy(t).start()
    g4[rep] = g3[...]
    g4_pair(chips - 1).start()
    for t in range(chips - 1):
        g4_copy(t).wait_recv()
        g4_pair(t).start()
    for t in range(chips):
        g4_pair(t).wait_recv()
    for index in range(rows_n):
        out = (gs_v, gn_v)[index * g_rows // width]
        low = index * g_rows % width
        for side in range(2):
            out[low : low + g_rows, side * half : (side + 1) * half] = g4[
                side * (reps_n // 2) : (side + 1) * (reps_n // 2), index
            ].reshape(g_rows, half)
    outs[1].start()
    outs[2].start()
    column_sums(1)
    outs[4].start()

    for far, step in row_steps:
        feature_copy(1, far, step).wait_send()
        g1_copy(far, step).wait_send()
        g3_copy(far, step).wait_send()
    for part in range(2):
        for t in range(chips):
            pair_copy(part, t).wait_send()
        for t in range(chips - 1):
            part_copy(part, t).wait_send()
        for t in range(rows_n - 1):
            back_copy(part, t).wait_send()
        for across in range(2):
            for along in range(ring):
                if across or along:
                    message_copy(part, across, along).wait_send()
                sibling_copy(part, across, along).wait_send()
    for step in range(1, reps_n):
        g2_copy(step).wait_send()
    for t in range(chips):
        if t < chips - 1:
            g4_copy(t).wait_send()
        g4_pair(t).wait_send()
    for copy in outs:
        copy.wait()


def store(*refs):
    count = len(refs) // 2
    sems = refs[-1]
    copies = [
        pltpu.make_async_copy(refs[index], refs[count + index], sems.at[index])
        for index in range(count)
    ]
    for copy in copies:
        copy.start()
    for copy in copies:
        copy.wait()


def per_device(
    features,
    self_weight,
    neigh_weight,
    out_bias,
    tile_masks,
    tile_live,
    tile_columns,
    node_degree,
    cotangent,
):
    rows_n = lax.axis_size("row")
    reps_n = lax.axis_size("rep")
    panel_rows, width = features.shape
    share = node_degree.shape[0]
    slots = tile_masks.shape[1]
    tile = tile_masks.shape[2]
    chips = reps_n // 2
    lanes = width // 2
    tile_rows = 2 * width // rows_n // (reps_n // 2)
    scale = 1.0 / math.sqrt(share * rows_n * reps_n)
    block = (share, width)
    anywhere = pl.BlockSpec(memory_space=pl.ANY)
    scalars = pl.BlockSpec(memory_space=pltpu.SMEM)
    dma = pltpu.SemaphoreType.DMA
    vmem = pltpu.VMEM
    grads = (reps_n + 2, tile_rows, lanes)
    half_block = (share, lanes)
    turned = (lanes, share)
    scratch = [
        vmem((panel_rows, slots * share), BF),
        vmem((BUFFERS, tile * slots, tile), jnp.int32),
        vmem((2, *block), BF),
        vmem((2, rows_n * share, lanes), BF),
        vmem((width, width), BF),
        vmem((width, width), BF),
        vmem((1, width), F32),
        vmem((1, share), jnp.int32),
        vmem(block, BF),
        vmem((2, 2, *half_block), F32),
        vmem((2, chips, *half_block), BF),
        vmem((2, chips, *half_block), BF),
        vmem((2, chips, *half_block), BF),
        vmem((2, chips, *half_block), BF),
        vmem((2, *half_block), F32),
        vmem(block, F32),
        vmem(block, BF),
        vmem((2, lanes, panel_rows), BF),
        vmem((2, *turned), F32),
        vmem((2, *turned), F32),
        vmem((2, rows_n, *turned), BF),
        vmem((2, rows_n, *turned), BF),
        vmem((rows_n, *grads), F32),
        vmem((rows_n, *grads), F32),
        vmem(grads, F32),
        vmem((reps_n, 3, tile_rows, lanes), F32),
        vmem((reps_n, 3, tile_rows, lanes), F32),
        vmem((rows_n, tile_rows, lanes), F32),
        vmem((reps_n, rows_n, tile_rows, lanes), F32),
        vmem(block, BF),
        vmem(block, BF),
        vmem((width, width), F32),
        vmem((width, width), F32),
        vmem((1, width), F32),
        dma((BUFFERS,)),
        dma((7,)),
        dma((5,)),
        dma((2, rows_n)),
        dma((2, rows_n)),
    ]
    scratch += [dma((2, chips))] * 8 + [dma((2, rows_n))] * 2 + [dma((rows_n,))] * 2
    scratch += [dma((reps_n,))] * 2 + [dma((rows_n,))] * 2 + [dma((chips,))] * 4
    results = pl.pallas_call(
        functools.partial(kernel, rows_n, reps_n, scale),
        out_shape=(
            jax.ShapeDtypeStruct(block, BF),
            jax.ShapeDtypeStruct(block, BF),
            jax.ShapeDtypeStruct((width, width), F32),
            jax.ShapeDtypeStruct((width, width), F32),
            jax.ShapeDtypeStruct((1, width), F32),
        ),
        in_specs=[anywhere] * 5 + [scalars] * 2 + [anywhere] * 2,
        out_specs=(anywhere,) * 5,
        scratch_shapes=scratch,
        compiler_params=pltpu.CompilerParams(
            collective_id=0, has_side_effects=True, vmem_limit_bytes=56 * 1024 * 1024
        ),
        name="layer",
    )(
        features,
        self_weight,
        neigh_weight,
        out_bias.reshape(1, width),
        tile_masks.reshape(panel_rows * slots, tile),
        tile_live.T,
        tile_columns.T,
        node_degree.reshape(1, share),
        cotangent,
    )
    hidden, grad_features, grad_self, grad_neigh, grad_bias = pl.pallas_call(
        store,
        out_shape=tuple(jax.ShapeDtypeStruct(one.shape, one.dtype) for one in results),
        in_specs=[anywhere] * 5,
        out_specs=(anywhere,) * 5,
        scratch_shapes=[dma((5,))],
        name="store",
    )(*results)
    return (hidden, grad_features, grad_self, grad_neigh, grad_bias.reshape(width))


def solution(mesh):
    return jax.shard_map(
        per_device,
        mesh=mesh,
        in_specs=(
            P("row", None),
            P(),
            P(),
            P(),
            P("row", "rep", None),
            P("row", "rep"),
            P("row", "rep"),
            P(("row", "rep")),
            P(("row", "rep"), None),
        ),
        out_specs=(P(("row", "rep"), None), P(("row", "rep"), None), P(), P(), P()),
        check_vma=False,
    )
```

```python
import functools
import math

import jax
import jax.numpy as jnp
from jax import lax
from jax.experimental import pallas as pl
from jax.experimental.pallas import tpu as pltpu
from jax.sharding import PartitionSpec as P

BF = jnp.bfloat16
F32 = jnp.float32
BUFFERS = 16
LAG = 2
CONTRACT_LAST = (((1,), (1,)), ((), ()))
CONTRACT_FIRST = (((0,), (0,)), ((), ()))


def kernel(
    rows_n,
    reps_n,
    scale,
    features,
    self_weight,
    neigh_weight,
    bias,
    masks,
    live_hbm,
    column_hbm,
    degree,
    cotangent,
    hidden_out,
    grad_features,
    grad_self,
    grad_neigh,
    grad_bias,
    live,
    column,
    dense,
    mask_buf,
    feat_v,
    gathered,
    sw_v,
    nw_v,
    bias_v,
    degree_v,
    cot_v,
    work,
    pair_send,
    pair_recv,
    part_send,
    part_recv,
    own_sum,
    pre_v,
    mean_v,
    msg_all,
    direct,
    back_own,
    back_send,
    back_recv,
    g1_send,
    g1_recv,
    g1_sum,
    g2_send,
    g2_recv,
    g3,
    g4,
    hid_v,
    gf_v,
    gs_v,
    gn_v,
    gb_v,
    mask_sem,
    in_sem,
    out_sem,
    s1,
    r1,
    s2p,
    r2p,
    s2,
    r2,
    s3,
    r3,
    s3f,
    r3f,
    s4,
    r4,
    sg1,
    rg1,
    sg2,
    rg2,
    sg3,
    rg3,
    sg4,
    rg4,
    sg4f,
    rg4f,
):
    width = self_weight.shape[0]
    share = cotangent.shape[0]
    half = width // 2
    tile = masks.shape[1]
    half_rows = rows_n // 2
    chips = reps_n // 2
    ring = chips // 2
    mask_rows = tile * rows_n
    blocks = masks.shape[0] // mask_rows
    slot_width = share
    row = lax.axis_index("row")
    rep = lax.axis_index("rep")
    core = lax.rem(rep, 2)
    chip = lax.div(rep, 2)
    row_far, row_step = lax.div(row, half_rows), lax.rem(row, half_rows)
    chip_across, chip_along = lax.div(chip, ring), lax.rem(chip, ring)
    sibling = chip * 2 + 1 - core
    far_rep = lax.rem(rep + reps_n // 2, reps_n)

    def remote(src, dst, send, recv, to_row, to_rep):
        return pltpu.make_async_remote_copy(
            src_ref=src,
            dst_ref=dst,
            send_sem=send,
            recv_sem=recv,
            device_id=(to_row, to_rep),
            device_id_type=pl.DeviceIdType.MESH,
        )

    def share_rows(index):
        return pl.ds(pl.multiple_of(index * share, share), share)

    def row_at(far, step):
        return lax.rem(row_far + far, 2) * half_rows + lax.rem(row_step + step, half_rows)

    def chip_at(across, along):
        return lax.rem(chip_across + across, 2) * ring + lax.rem(chip_along + along, ring)

    def chip_from(across, along):
        return lax.rem(chip_across + across, 2) * ring + lax.rem(chip_along + ring - along, ring)

    def offset(t, size):
        if isinstance(t, int):
            across, turn = (t + 1) % 2, t // 2
            return across, (1 + turn if across else size - 1 - turn) % size
        across, turn = lax.rem(t + 1, 2), lax.div(t, 2)
        return across, lax.rem(across * (1 + turn) + (1 - across) * (size - 1 - turn), size)

    row_steps = [
        (far, step) for step in range(half_rows) for far in range(2) if (far, step) != (0, 0)
    ]

    def mask_copy(block, slot):
        return pltpu.make_async_copy(
            masks.at[pl.ds(pl.multiple_of(block * mask_rows, mask_rows), mask_rows), :],
            mask_buf.at[slot],
            mask_sem.at[slot],
        )

    def greet(to_row, to_rep):
        pl.semaphore_signal(
            barrier, inc=1, device_id=(to_row, to_rep), device_id_type=pl.DeviceIdType.MESH
        )

    barrier = pltpu.get_barrier_semaphore()
    greeted = 0
    for far, step in row_steps:
        greet(row_at(far, step), rep)
        greeted += 1
        if far:
            greet(row_at(far, step), far_rep)
            greeted += 1
    for step in range(1, reps_n):
        greet(row, lax.rem(rep + step, reps_n))
        greeted += 1

    inputs = [
        pltpu.make_async_copy(src, dst, in_sem.at[index])
        for index, (src, dst) in enumerate(
            (
                (features.at[share_rows(rep), :], feat_v.at[0]),
                (features.at[share_rows(far_rep), :], feat_v.at[1]),
                (live_hbm, live),
                (column_hbm, column),
                (self_weight, sw_v),
                (neigh_weight, nw_v),
                (bias, bias_v),
                (degree, degree_v),
                (cotangent, cot_v),
            )
        )
    ]
    for copy in inputs[:4]:
        copy.start()

    def expand(block, carry):
        slot = lax.rem(block, BUFFERS)
        mask_copy(block, slot).wait()
        at = pl.ds(pl.multiple_of(block * tile, tile), tile)
        for s in range(rows_n):
            bits = mask_buf[slot, pl.ds(s, tile, stride=rows_n), :].astype(F32)
            held = live[s, block].astype(F32)
            second = held * column[s, block].astype(F32)
            first = held - second
            dense[at, s * slot_width : s * slot_width + tile] = (bits * first).astype(BF)
            dense[at, s * slot_width + tile : (s + 1) * slot_width] = (bits * second).astype(BF)

        @pl.when(block + BUFFERS < blocks)
        def _():
            mask_copy(block + BUFFERS, slot).start()

        return carry

    def feature_copy(part, far, step):
        return remote(
            feat_v.at[far, :, part * half : (part + 1) * half],
            gathered.at[part, share_rows(row), :],
            s1.at[part, far * half_rows + step],
            r1.at[part, far * half_rows + step],
            row_at(far, step),
            far_rep if far else rep,
        )

    for copy in inputs[:4]:
        copy.wait()
    pl.semaphore_wait(barrier, greeted)
    for far, step in row_steps:
        feature_copy(0, far, step).start()
    for block in range(BUFFERS):
        mask_copy(block, block).start()
    for copy in inputs[4:]:
        copy.start()
    lax.fori_loop(0, blocks, expand, 0)
    for copy in inputs[4:]:
        copy.wait()
    for part in range(2):
        gathered[part, share_rows(row), :] = feat_v[0, :, part * half : (part + 1) * half]
    own = feat_v[0]
    pre_v[...] = jnp.dot(own, sw_v[...], preferred_element_type=F32) + bias_v[...]
    degree_row = degree_v[...].astype(F32)
    degree_column = jnp.transpose(jnp.broadcast_to(degree_row, (half, share)))
    for far, step in row_steps:
        feature_copy(0, far, step).wait_send()
    for far, step in row_steps:
        feature_copy(1, far, step).start()

    def pair_copy(part, t):
        return remote(
            pair_send.at[part, t],
            pair_recv.at[part, t],
            s2p.at[part, t],
            r2p.at[part, t],
            row,
            sibling,
        )

    def part_copy(part, t):
        return remote(
            part_send.at[part, t],
            part_recv.at[part, t],
            s2.at[part, t],
            r2.at[part, t],
            row,
            chip_at(*offset(t, ring)) * 2 + core,
        )

    def finish_pair(part, t):
        pair_copy(part, t).wait_recv()
        part_send[part, t] = (work[t % 4 if isinstance(t, int) else lax.rem(t, 4), core] + pair_recv[part, t].astype(F32)).astype(BF)
        part_copy(part, t).start()

    def forward(part):
        def body(t, carry):
            at = chip_at(*offset(t, ring))
            rows = pl.ds(pl.multiple_of(at * (2 * share), 2 * share), 2 * share)
            work[lax.rem(t, 4)] = jnp.dot(
                dense[rows, :], gathered[part], preferred_element_type=F32
            ).reshape(2, share, half)
            pair_send[part, t] = work[lax.rem(t, 4), 1 - core].astype(BF)
            pair_copy(part, t).start()

            @pl.when(t >= LAG)
            def _():
                finish_pair(part, t - LAG)

            return carry

        for far, step in row_steps:
            feature_copy(part, far, step).wait_recv()
        lax.fori_loop(0, chips, body, 0)
        for t in range(max(chips - LAG, 0), chips - 1):
            finish_pair(part, t)
        pair_copy(part, chips - 1).wait_recv()
        own_sum[part] = work[(chips - 1) % 4, core] + pair_recv[part, chips - 1].astype(F32)

    forward(0)
    forward(1)
    for part in range(2):
        total = own_sum[part]
        for t in range(chips - 1):
            part_copy(part, t).wait_recv()
            total = total + part_recv[part, t].astype(F32)
        mean = (total / degree_column).astype(BF)
        mean_v[:, part * half : (part + 1) * half] = mean
        pre_v[...] += jnp.dot(
            mean, nw_v[part * half : (part + 1) * half, :], preferred_element_type=F32
        )

    pre = pre_v[...]
    root = math.sqrt(2.0 / math.pi)
    square = pre * pre
    bend = jnp.tanh(root * (pre + 0.044715 * (square * pre)))
    slope = 0.5 * (1.0 + bend) + (0.5 * root) * pre * (1.0 - bend * bend) * (
        1.0 + (3.0 * 0.044715) * square
    )
    dpre = cot_v[...].astype(F32) * slope
    dpre_b = dpre.astype(BF)

    def message_copy(part, across, along):
        relay = across and along
        source = (chip_at(1, 0) if relay else chip) * 2 + core
        place = msg_all.at[part, :, share_rows(source)]
        index = across * ring + along
        target = chip_at(0 if relay else across, along) * 2 + core
        return remote(place, place, s3.at[part, index], r3.at[part, index], row, target)

    def sibling_copy(part, across, along):
        place = msg_all.at[part, :, share_rows(chip_from(across, along) * 2 + core)]
        index = across * ring + along
        return remote(place, place, s3f.at[part, index], r3f.at[part, index], row, sibling)

    along_order = sorted(range(1, ring), key=lambda d: min(d, ring - d))

    def send_messages(part):
        message_copy(part, 1, 0).start()
        for along in along_order:
            message_copy(part, 0, along).start()
        sibling_copy(part, 0, 0).start()

    def relay_messages(part):
        message_copy(part, 1, 0).wait_recv()
        for along in along_order:
            message_copy(part, 1, along).start()
        sibling_copy(part, 1, 0).start()

    def finish_messages(part):
        for across in range(2):
            for along in along_order:
                message_copy(part, across, along).wait_recv()
                sibling_copy(part, across, along).start()
        for across in range(2):
            for along in range(ring):
                sibling_copy(part, across, along).wait_recv()

    for part in range(2):
        msg_all[part, :, share_rows(rep)] = (
            lax.dot_general(
                nw_v[part * half : (part + 1) * half, :],
                dpre_b,
                CONTRACT_LAST,
                preferred_element_type=F32,
            )
            / degree_row
        ).astype(BF)
        if part == 0:
            send_messages(0)

    outs = [
        pltpu.make_async_copy(src, dst, out_sem.at[index])
        for index, (src, dst) in enumerate(
            (
                (hid_v, hidden_out),
                (gs_v, grad_self),
                (gn_v, grad_neigh),
                (gb_v, grad_bias),
                (gf_v, grad_features),
            )
        )
    ]
    hid_v[...] = (0.5 * pre * (1.0 + bend)).astype(BF)
    outs[0].start()

    g_rows = 2 * width // rows_n
    tile_rows = g_rows // (reps_n // 2)
    terms = [
        lax.dot_general(left, dpre_b, CONTRACT_FIRST, preferred_element_type=F32) * scale
        for left in (feat_v[0], mean_v[...])
    ]
    bias_term = jnp.sum(dpre, axis=0, keepdims=True) * scale
    for index in range(rows_n):
        term = terms[index * g_rows // width]
        low = index * g_rows % width
        for side in range(2):
            g1_send[index, side * (reps_n // 2) : (side + 1) * (reps_n // 2)] = term[
                low : low + g_rows, side * half : (side + 1) * half
            ].reshape(reps_n // 2, tile_rows, half)
            g1_send[index, reps_n + side] = jnp.broadcast_to(
                bias_term[:, side * half : (side + 1) * half], (tile_rows, half)
            )

    def g1_copy(far, step):
        index = far * half_rows + step
        to_row = row_at(far, step)
        return remote(
            g1_send.at[to_row],
            g1_recv.at[index],
            sg1.at[index],
            rg1.at[index],
            to_row,
            far_rep if far else rep,
        )

    for far, step in row_steps:
        g1_copy(far, step).start()
    direct[...] = lax.dot_general(
        sw_v[...], dpre_b, CONTRACT_LAST, preferred_element_type=F32
    ).reshape(2, half, share)

    def back_copy(part, t):
        return remote(
            back_send.at[part, t],
            back_recv.at[part, t],
            s4.at[part, t],
            r4.at[part, t],
            row_at(*offset(t, half_rows)),
            rep,
        )

    def backward(part, low, high):
        def body(t, carry):
            target = row_at(*offset(t, half_rows))
            columns = pl.ds(pl.multiple_of(target * slot_width, slot_width), slot_width)
            term = jnp.dot(msg_all[part], dense[:, columns], preferred_element_type=F32)

            @pl.when(t < rows_n - 1)
            def _():
                back_send[part, t] = term.astype(BF)
                back_copy(part, t).start()

            @pl.when(t == rows_n - 1)
            def _():
                back_own[part] = term

            return carry

        lax.fori_loop(low, high, body, 0)

    relay_messages(0)
    finish_messages(0)
    def g2_copy(step):
        to_rep = lax.rem(rep + step, reps_n)
        return remote(g2_send.at[to_rep], g2_recv.at[step], sg2.at[step], rg2.at[step], row, to_rep)

    def g3_copy(far, step):
        index = far * half_rows + step
        return remote(g3.at[row], g3.at[row], sg3.at[index], rg3.at[index], row_at(far, step), rep)

    def g4_copy(t):
        return remote(
            g3, g4.at[rep], sg4.at[t], rg4.at[t], row, chip_at(*offset(t, ring)) * 2 + core
        )

    def g4_pair(t):
        source = chip_from(*offset(t, ring)) * 2 + core
        return remote(g4.at[source], g4.at[source], sg4f.at[t], rg4f.at[t], row, sibling)

    send_messages(1)
    backward(0, 0, rows_n // 2)
    total = g1_send[row]
    for far, step in row_steps:
        g1_copy(far, step).wait_recv()
        total = total + g1_recv[far * half_rows + step]
    g1_sum[...] = total
    for index in range(reps_n):
        g2_send[index, 0] = g1_sum[index]
        g2_send[index, 1] = g1_sum[reps_n]
        g2_send[index, 2] = g1_sum[reps_n + 1]
    for step in range(1, reps_n):
        g2_copy(step).start()
    relay_messages(1)
    backward(0, rows_n // 2, rows_n)
    total = g2_send[rep]
    for step in range(1, reps_n):
        g2_copy(step).wait_recv()
        total = total + g2_recv[step]
    g3[row] = total[0]
    for far, step in row_steps:
        g3_copy(far, step).start()
    for side in range(2):
        gb_v[:, side * half : (side + 1) * half] = total[1 + side][0:1, :]
    outs[3].start()
    finish_messages(1)
    backward(1, 0, rows_n // 2)
    for far, step in row_steps:
        g3_copy(far, step).wait_recv()
    for t in range(chips - 1):
        g4_copy(t).start()
    g4[rep] = g3[...]
    g4_pair(chips - 1).start()
    backward(1, rows_n // 2, rows_n)

    def column_sums(part):
        total = direct[part] + back_own[part]
        for t in range(rows_n - 1):
            back_copy(part, t).wait_recv()
            total = total + back_recv[part, t].astype(F32)
        gf_v[:, part * half : (part + 1) * half] = jnp.transpose(total).astype(BF)

    column_sums(0)
    for t in range(chips - 1):
        g4_copy(t).wait_recv()
        g4_pair(t).start()
    for t in range(chips):
        g4_pair(t).wait_recv()
    for index in range(rows_n):
        out = (gs_v, gn_v)[index * g_rows // width]
        low = index * g_rows % width
        for side in range(2):
            out[low : low + g_rows, side * half : (side + 1) * half] = g4[
                side * (reps_n // 2) : (side + 1) * (reps_n // 2), index
            ].reshape(g_rows, half)
    outs[1].start()
    outs[2].start()
    column_sums(1)
    outs[4].start()

    for far, step in row_steps:
        feature_copy(1, far, step).wait_send()
        g1_copy(far, step).wait_send()
        g3_copy(far, step).wait_send()
    for part in range(2):
        for t in range(chips):
            pair_copy(part, t).wait_send()
        for t in range(chips - 1):
            part_copy(part, t).wait_send()
        for t in range(rows_n - 1):
            back_copy(part, t).wait_send()
        for across in range(2):
            for along in range(ring):
                if across or along:
                    message_copy(part, across, along).wait_send()
                sibling_copy(part, across, along).wait_send()
    for step in range(1, reps_n):
        g2_copy(step).wait_send()
    for t in range(chips):
        if t < chips - 1:
            g4_copy(t).wait_send()
        g4_pair(t).wait_send()
    for copy in outs:
        copy.wait()


def store(*refs):
    count = (len(refs) - 2) // 3
    given, results, staged = refs[:count], refs[count : 2 * count], refs[2 * count : 3 * count]
    arrived, left = refs[3 * count :]
    inward = [
        pltpu.make_async_copy(given[index], staged[index], arrived.at[index])
        for index in range(count)
    ]
    outward = [
        pltpu.make_async_copy(staged[index], results[index], left.at[index])
        for index in range(count)
    ]
    for copy in inward:
        copy.start()
    for index in range(count):
        inward[index].wait()
        outward[index].start()
    for copy in outward:
        copy.wait()


def per_device(
    features,
    self_weight,
    neigh_weight,
    out_bias,
    tile_masks,
    tile_live,
    tile_columns,
    node_degree,
    cotangent,
):
    rows_n = lax.axis_size("row")
    reps_n = lax.axis_size("rep")
    panel_rows, width = features.shape
    share = node_degree.shape[0]
    slots = tile_masks.shape[1]
    tile = tile_masks.shape[2]
    chips = reps_n // 2
    lanes = width // 2
    tile_rows = 2 * width // rows_n // (reps_n // 2)
    scale = 1.0 / math.sqrt(share * rows_n * reps_n)
    block = (share, width)
    anywhere = pl.BlockSpec(memory_space=pl.ANY)
    dma = pltpu.SemaphoreType.DMA
    vmem = pltpu.VMEM
    grads = (reps_n + 2, tile_rows, lanes)
    half_block = (share, lanes)
    turned = (lanes, share)
    scratch = [
        pltpu.SMEM((slots, panel_rows // tile), jnp.int32),
        pltpu.SMEM((slots, panel_rows // tile), jnp.int32),
        vmem((panel_rows, slots * share), BF),
        vmem((BUFFERS, tile * slots, tile), jnp.int32),
        vmem((2, *block), BF),
        vmem((2, rows_n * share, lanes), BF),
        vmem((width, width), BF),
        vmem((width, width), BF),
        vmem((1, width), F32),
        vmem((1, share), jnp.int32),
        vmem(block, BF),
        vmem((4, 2, *half_block), F32),
        vmem((2, chips, *half_block), BF),
        vmem((2, chips, *half_block), BF),
        vmem((2, chips, *half_block), BF),
        vmem((2, chips, *half_block), BF),
        vmem((2, *half_block), F32),
        vmem(block, F32),
        vmem(block, BF),
        vmem((2, lanes, panel_rows), BF),
        vmem((2, *turned), F32),
        vmem((2, *turned), F32),
        vmem((2, rows_n, *turned), BF),
        vmem((2, rows_n, *turned), BF),
        vmem((rows_n, *grads), F32),
        vmem((rows_n, *grads), F32),
        vmem(grads, F32),
        vmem((reps_n, 3, tile_rows, lanes), F32),
        vmem((reps_n, 3, tile_rows, lanes), F32),
        vmem((rows_n, tile_rows, lanes), F32),
        vmem((reps_n, rows_n, tile_rows, lanes), F32),
        vmem(block, BF),
        vmem(block, BF),
        vmem((width, width), F32),
        vmem((width, width), F32),
        vmem((1, width), F32),
        dma((BUFFERS,)),
        dma((9,)),
        dma((5,)),
        dma((2, rows_n)),
        dma((2, rows_n)),
    ]
    scratch += [dma((2, chips))] * 8 + [dma((2, rows_n))] * 2 + [dma((rows_n,))] * 2
    scratch += [dma((reps_n,))] * 2 + [dma((rows_n,))] * 2 + [dma((chips,))] * 4
    results = pl.pallas_call(
        functools.partial(kernel, rows_n, reps_n, scale),
        out_shape=(
            jax.ShapeDtypeStruct(block, BF),
            jax.ShapeDtypeStruct(block, BF),
            jax.ShapeDtypeStruct((width, width), F32),
            jax.ShapeDtypeStruct((width, width), F32),
            jax.ShapeDtypeStruct((1, width), F32),
        ),
        in_specs=[anywhere] * 9,
        out_specs=(anywhere,) * 5,
        scratch_shapes=scratch,
        compiler_params=pltpu.CompilerParams(
            collective_id=0, has_side_effects=True, vmem_limit_bytes=56 * 1024 * 1024
        ),
        name="layer",
    )(
        features,
        self_weight,
        neigh_weight,
        out_bias.reshape(1, width),
        tile_masks.reshape(panel_rows * slots, tile),
        tile_live.T,
        tile_columns.T,
        node_degree.reshape(1, share),
        cotangent,
    )
    hidden, grad_features, grad_self, grad_neigh, grad_bias = pl.pallas_call(
        store,
        out_shape=tuple(jax.ShapeDtypeStruct(one.shape, one.dtype) for one in results),
        in_specs=[anywhere] * 5,
        out_specs=(anywhere,) * 5,
        scratch_shapes=[vmem(one.shape, one.dtype) for one in results] + [dma((5,))] * 2,
        name="store",
    )(*results)
    return (hidden, grad_features, grad_self, grad_neigh, grad_bias.reshape(width))


def solution(mesh):
    return jax.shard_map(
        per_device,
        mesh=mesh,
        in_specs=(
            P("row", None),
            P(),
            P(),
            P(),
            P("row", "rep", None),
            P("row", "rep"),
            P("row", "rep"),
            P(("row", "rep")),
            P(("row", "rep"), None),
        ),
        out_specs=(P(("row", "rep"), None), P(("row", "rep"), None), P(), P(), P()),
        check_vma=False,
    )
```

```python
import functools
import math

import jax
import jax.numpy as jnp
from jax import lax
from jax.experimental import pallas as pl
from jax.experimental.pallas import tpu as pltpu
from jax.sharding import PartitionSpec as P

BF = jnp.bfloat16
F32 = jnp.float32
BUFFERS = 16
LAG = 2
CONTRACT_LAST = (((1,), (1,)), ((), ()))
CONTRACT_FIRST = (((0,), (0,)), ((), ()))


def kernel(
    rows_n,
    reps_n,
    scale,
    features,
    self_weight,
    neigh_weight,
    bias,
    masks,
    live_hbm,
    column_hbm,
    degree,
    cotangent,
    hid_v,
    gf_v,
    gs_v,
    gn_v,
    gb_v,
    live,
    column,
    dense,
    mask_buf,
    feat_v,
    gathered,
    sw_v,
    nw_v,
    bias_v,
    degree_v,
    cot_v,
    work,
    pair_send,
    pair_recv,
    part_send,
    part_recv,
    own_sum,
    pre_v,
    mean_v,
    msg_all,
    direct,
    back_own,
    back_send,
    back_recv,
    g1_send,
    g1_recv,
    g1_sum,
    g2_send,
    g2_recv,
    g3,
    g4,
    mask_sem,
    in_sem,
    s1,
    r1,
    s2p,
    r2p,
    s2,
    r2,
    s3,
    r3,
    s3f,
    r3f,
    s4,
    r4,
    sg1,
    rg1,
    sg2,
    rg2,
    sg3,
    rg3,
    sg4,
    rg4,
    sg4f,
    rg4f,
):
    width = self_weight.shape[0]
    share = cotangent.shape[0]
    half = width // 2
    tile = masks.shape[1]
    half_rows = rows_n // 2
    chips = reps_n // 2
    ring = chips // 2
    mask_rows = tile * rows_n
    blocks = masks.shape[0] // mask_rows
    slot_width = share
    row = lax.axis_index("row")
    rep = lax.axis_index("rep")
    core = lax.rem(rep, 2)
    chip = lax.div(rep, 2)
    row_far, row_step = lax.div(row, half_rows), lax.rem(row, half_rows)
    chip_across, chip_along = lax.div(chip, ring), lax.rem(chip, ring)
    sibling = chip * 2 + 1 - core
    far_rep = lax.rem(rep + reps_n // 2, reps_n)

    def remote(src, dst, send, recv, to_row, to_rep):
        return pltpu.make_async_remote_copy(
            src_ref=src,
            dst_ref=dst,
            send_sem=send,
            recv_sem=recv,
            device_id=(to_row, to_rep),
            device_id_type=pl.DeviceIdType.MESH,
        )

    def share_rows(index):
        return pl.ds(pl.multiple_of(index * share, share), share)

    def row_at(far, step):
        return lax.rem(row_far + far, 2) * half_rows + lax.rem(row_step + step, half_rows)

    def chip_at(across, along):
        return lax.rem(chip_across + across, 2) * ring + lax.rem(chip_along + along, ring)

    def chip_from(across, along):
        return lax.rem(chip_across + across, 2) * ring + lax.rem(chip_along + ring - along, ring)

    def offset(t, size):
        if isinstance(t, int):
            across, turn = (t + 1) % 2, t // 2
            return across, (1 + turn if across else size - 1 - turn) % size
        across, turn = lax.rem(t + 1, 2), lax.div(t, 2)
        return across, lax.rem(across * (1 + turn) + (1 - across) * (size - 1 - turn), size)

    row_steps = [
        (far, step) for step in range(half_rows) for far in range(2) if (far, step) != (0, 0)
    ]

    def mask_copy(block, slot):
        return pltpu.make_async_copy(
            masks.at[pl.ds(pl.multiple_of(block * mask_rows, mask_rows), mask_rows), :],
            mask_buf.at[slot],
            mask_sem.at[slot],
        )

    def greet(to_row, to_rep):
        pl.semaphore_signal(
            barrier, inc=1, device_id=(to_row, to_rep), device_id_type=pl.DeviceIdType.MESH
        )

    barrier = pltpu.get_barrier_semaphore()
    greeted = 0
    for far, step in row_steps:
        greet(row_at(far, step), rep)
        greeted += 1
        if far:
            greet(row_at(far, step), far_rep)
            greeted += 1
    for step in range(1, reps_n):
        greet(row, lax.rem(rep + step, reps_n))
        greeted += 1

    inputs = [
        pltpu.make_async_copy(src, dst, in_sem.at[index])
        for index, (src, dst) in enumerate(
            (
                (features.at[share_rows(rep), :], feat_v.at[0]),
                (features.at[share_rows(far_rep), :], feat_v.at[1]),
                (live_hbm, live),
                (column_hbm, column),
                (self_weight, sw_v),
                (neigh_weight, nw_v),
                (bias, bias_v),
                (degree, degree_v),
                (cotangent, cot_v),
            )
        )
    ]
    for copy in inputs[:4]:
        copy.start()

    def expand(block, carry):
        slot = lax.rem(block, BUFFERS)
        mask_copy(block, slot).wait()
        at = pl.ds(pl.multiple_of(block * tile, tile), tile)
        for s in range(rows_n):
            bits = mask_buf[slot, pl.ds(s, tile, stride=rows_n), :].astype(F32)
            held = live[s, block].astype(F32)
            second = held * column[s, block].astype(F32)
            first = held - second
            dense[at, s * slot_width : s * slot_width + tile] = (bits * first).astype(BF)
            dense[at, s * slot_width + tile : (s + 1) * slot_width] = (bits * second).astype(BF)

        @pl.when(block + BUFFERS < blocks)
        def _():
            mask_copy(block + BUFFERS, slot).start()

        return carry

    def feature_copy(part, far, step):
        return remote(
            feat_v.at[far, :, part * half : (part + 1) * half],
            gathered.at[part, share_rows(row), :],
            s1.at[part, far * half_rows + step],
            r1.at[part, far * half_rows + step],
            row_at(far, step),
            far_rep if far else rep,
        )

    for copy in inputs[:4]:
        copy.wait()
    pl.semaphore_wait(barrier, greeted)
    for far, step in row_steps:
        feature_copy(0, far, step).start()
    for block in range(BUFFERS):
        mask_copy(block, block).start()
    for copy in inputs[4:]:
        copy.start()
    early = blocks - blocks // 5
    lax.fori_loop(0, early, expand, 0)
    for far, step in row_steps:
        feature_copy(0, far, step).wait_send()
    for far, step in row_steps:
        feature_copy(1, far, step).start()
    lax.fori_loop(early, blocks, expand, 0)
    for copy in inputs[4:]:
        copy.wait()
    for part in range(2):
        gathered[part, share_rows(row), :] = feat_v[0, :, part * half : (part + 1) * half]
    own = feat_v[0]
    pre_v[...] = jnp.dot(own, sw_v[...], preferred_element_type=F32) + bias_v[...]
    degree_row = degree_v[...].astype(F32)
    degree_column = jnp.transpose(jnp.broadcast_to(degree_row, (half, share)))

    def pair_copy(part, t):
        return remote(
            pair_send.at[part, t],
            pair_recv.at[part, t],
            s2p.at[part, t],
            r2p.at[part, t],
            row,
            sibling,
        )

    def part_copy(part, t):
        return remote(
            part_send.at[part, t],
            part_recv.at[part, t],
            s2.at[part, t],
            r2.at[part, t],
            row,
            chip_at(*offset(t, ring)) * 2 + core,
        )

    def finish_pair(part, t):
        pair_copy(part, t).wait_recv()
        part_send[part, t] = (work[t % 4 if isinstance(t, int) else lax.rem(t, 4), core] + pair_recv[part, t].astype(F32)).astype(BF)
        part_copy(part, t).start()

    def forward(part):
        def body(t, carry):
            at = chip_at(*offset(t, ring))
            rows = pl.ds(pl.multiple_of(at * (2 * share), 2 * share), 2 * share)
            work[lax.rem(t, 4)] = jnp.dot(
                dense[rows, :], gathered[part], preferred_element_type=F32
            ).reshape(2, share, half)
            pair_send[part, t] = work[lax.rem(t, 4), 1 - core].astype(BF)
            pair_copy(part, t).start()

            @pl.when(t >= LAG)
            def _():
                finish_pair(part, t - LAG)

            return carry

        for far, step in row_steps:
            feature_copy(part, far, step).wait_recv()
        lax.fori_loop(0, chips, body, 0)
        for t in range(max(chips - LAG, 0), chips - 1):
            finish_pair(part, t)
        pair_copy(part, chips - 1).wait_recv()
        own_sum[part] = work[(chips - 1) % 4, core] + pair_recv[part, chips - 1].astype(F32)

    forward(0)
    forward(1)
    for part in range(2):
        total = own_sum[part]
        for t in range(chips - 1):
            part_copy(part, t).wait_recv()
            total = total + part_recv[part, t].astype(F32)
        mean = (total / degree_column).astype(BF)
        mean_v[:, part * half : (part + 1) * half] = mean
        pre_v[...] += jnp.dot(
            mean, nw_v[part * half : (part + 1) * half, :], preferred_element_type=F32
        )

    pre = pre_v[...]
    root = math.sqrt(2.0 / math.pi)
    square = pre * pre
    bend = jnp.tanh(root * (pre + 0.044715 * (square * pre)))
    slope = 0.5 * (1.0 + bend) + (0.5 * root) * pre * (1.0 - bend * bend) * (
        1.0 + (3.0 * 0.044715) * square
    )
    dpre = cot_v[...].astype(F32) * slope
    dpre_b = dpre.astype(BF)

    def message_copy(part, across, along):
        relay = relayed(part, across, along)
        source = (chip_at(1, 0) if relay else chip) * 2 + core
        place = msg_all.at[part, :, share_rows(source)]
        index = across * ring + along
        target = chip_at(0 if relay else across, along) * 2 + core
        return remote(place, place, s3.at[part, index], r3.at[part, index], row, target)

    def sibling_copy(part, across, along):
        place = msg_all.at[part, :, share_rows(chip_from(across, along) * 2 + core)]
        index = across * ring + along
        return remote(place, place, s3f.at[part, index], r3f.at[part, index], row, sibling)

    along_order = sorted(range(1, ring), key=lambda d: min(d, ring - d))

    def relayed(part, across, along):
        return across == 1 and along > 0 and (part == 1 or along == ring // 2)

    own_first = [(1, 0)] + [
        (across, along)
        for along in along_order
        for across in range(2)
        if not relayed(0, across, along)
    ]
    relay_first = [(1, along) for along in along_order if relayed(0, 1, along)]
    all_second = [(across, along) for along in along_order for across in range(2)]

    def finish_messages(part):
        for across in range(2):
            for along in along_order:
                message_copy(part, across, along).wait_recv()
                sibling_copy(part, across, along).start()
        for across in range(2):
            for along in range(ring):
                sibling_copy(part, across, along).wait_recv()

    for part in range(2):
        msg_all[part, :, share_rows(rep)] = (
            lax.dot_general(
                nw_v[part * half : (part + 1) * half, :],
                dpre_b,
                CONTRACT_LAST,
                preferred_element_type=F32,
            )
            / degree_row
        ).astype(BF)
        if part == 0:
            for offsets in own_first:
                message_copy(0, *offsets).start()
            sibling_copy(0, 0, 0).start()
        else:
            message_copy(1, 1, 0).start()
            sibling_copy(1, 0, 0).start()

    hid_v[...] = (0.5 * pre * (1.0 + bend)).astype(BF)

    g_rows = 2 * width // rows_n
    tile_rows = g_rows // (reps_n // 2)
    terms = [
        lax.dot_general(left, dpre_b, CONTRACT_FIRST, preferred_element_type=F32) * scale
        for left in (feat_v[0], mean_v[...])
    ]
    bias_term = jnp.sum(dpre, axis=0, keepdims=True) * scale
    for index in range(rows_n):
        term = terms[index * g_rows // width]
        low = index * g_rows % width
        for side in range(2):
            g1_send[index, side * (reps_n // 2) : (side + 1) * (reps_n // 2)] = term[
                low : low + g_rows, side * half : (side + 1) * half
            ].reshape(reps_n // 2, tile_rows, half)
            g1_send[index, reps_n + side] = jnp.broadcast_to(
                bias_term[:, side * half : (side + 1) * half], (tile_rows, half)
            )

    def g1_copy(far, step):
        index = far * half_rows + step
        to_row = row_at(far, step)
        return remote(
            g1_send.at[to_row],
            g1_recv.at[index],
            sg1.at[index],
            rg1.at[index],
            to_row,
            far_rep if far else rep,
        )

    for far, step in row_steps:
        g1_copy(far, step).start()
    direct[...] = lax.dot_general(
        sw_v[...], dpre_b, CONTRACT_LAST, preferred_element_type=F32
    ).reshape(2, half, share)

    def back_copy(part, t):
        return remote(
            back_send.at[part, t],
            back_recv.at[part, t],
            s4.at[part, t],
            r4.at[part, t],
            row_at(*offset(t, half_rows)),
            rep,
        )

    def backward(part, low, high):
        def body(t, carry):
            target = row_at(*offset(t, half_rows))
            columns = pl.ds(pl.multiple_of(target * slot_width, slot_width), slot_width)
            term = jnp.dot(msg_all[part], dense[:, columns], preferred_element_type=F32)

            @pl.when(t < rows_n - 1)
            def _():
                back_send[part, t] = term.astype(BF)
                back_copy(part, t).start()

            @pl.when(t == rows_n - 1)
            def _():
                back_own[part] = term

            return carry

        lax.fori_loop(low, high, body, 0)

    message_copy(0, 1, 0).wait_recv()
    for offsets in relay_first:
        message_copy(0, *offsets).start()
    sibling_copy(0, 1, 0).start()
    for offsets in own_first:
        message_copy(0, *offsets).wait_send()
    message_copy(1, 1, 0).wait_recv()
    for offsets in all_second:
        message_copy(1, *offsets).start()
    sibling_copy(1, 1, 0).start()
    finish_messages(0)
    def g2_copy(step):
        to_rep = lax.rem(rep + step, reps_n)
        return remote(g2_send.at[to_rep], g2_recv.at[step], sg2.at[step], rg2.at[step], row, to_rep)

    def g3_copy(far, step):
        index = far * half_rows + step
        return remote(g3.at[row], g3.at[row], sg3.at[index], rg3.at[index], row_at(far, step), rep)

    def g4_copy(t):
        return remote(
            g3, g4.at[rep], sg4.at[t], rg4.at[t], row, chip_at(*offset(t, ring)) * 2 + core
        )

    def g4_pair(t):
        source = chip_from(*offset(t, ring)) * 2 + core
        return remote(g4.at[source], g4.at[source], sg4f.at[t], rg4f.at[t], row, sibling)

    backward(0, 0, rows_n // 4)
    total = g1_send[row]
    for far, step in row_steps:
        g1_copy(far, step).wait_recv()
        total = total + g1_recv[far * half_rows + step]
    g1_sum[...] = total
    for index in range(reps_n):
        g2_send[index, 0] = g1_sum[index]
        g2_send[index, 1] = g1_sum[reps_n]
        g2_send[index, 2] = g1_sum[reps_n + 1]
    for step in range(1, reps_n):
        g2_copy(step).start()
    backward(0, rows_n // 4, rows_n)
    total = g2_send[rep]
    for step in range(1, reps_n):
        g2_copy(step).wait_recv()
        total = total + g2_recv[step]
    g3[row] = total[0]
    for far, step in row_steps:
        g3_copy(far, step).start()
    for side in range(2):
        gb_v[:, side * half : (side + 1) * half] = total[1 + side][0:1, :]
    finish_messages(1)
    backward(1, 0, rows_n // 2)
    for far, step in row_steps:
        g3_copy(far, step).wait_recv()
    for t in range(chips - 1):
        g4_copy(t).start()
    g4[rep] = g3[...]
    g4_pair(chips - 1).start()
    backward(1, rows_n // 2, rows_n)

    def column_sums(part):
        total = direct[part] + back_own[part]
        for t in range(rows_n - 1):
            back_copy(part, t).wait_recv()
            total = total + back_recv[part, t].astype(F32)
        gf_v[:, part * half : (part + 1) * half] = jnp.transpose(total).astype(BF)

    column_sums(0)
    for t in range(chips - 1):
        g4_copy(t).wait_recv()
        g4_pair(t).start()
    for t in range(chips):
        g4_pair(t).wait_recv()
    for index in range(rows_n):
        out = (gs_v, gn_v)[index * g_rows // width]
        low = index * g_rows % width
        for side in range(2):
            out[low : low + g_rows, side * half : (side + 1) * half] = g4[
                side * (reps_n // 2) : (side + 1) * (reps_n // 2), index
            ].reshape(g_rows, half)
    column_sums(1)

    for far, step in row_steps:
        feature_copy(1, far, step).wait_send()
        g1_copy(far, step).wait_send()
        g3_copy(far, step).wait_send()
    for part in range(2):
        for t in range(chips):
            pair_copy(part, t).wait_send()
        for t in range(chips - 1):
            part_copy(part, t).wait_send()
        for t in range(rows_n - 1):
            back_copy(part, t).wait_send()
        for across in range(2):
            for along in range(ring):
                if (across or along) and not (part == 0 and (across, along) in own_first):
                    message_copy(part, across, along).wait_send()
                sibling_copy(part, across, along).wait_send()
    for step in range(1, reps_n):
        g2_copy(step).wait_send()
    for t in range(chips):
        if t < chips - 1:
            g4_copy(t).wait_send()
        g4_pair(t).wait_send()


def store(*refs):
    count = len(refs) // 2
    sems = refs[-1]
    copies = [
        pltpu.make_async_copy(refs[index], refs[count + index], sems.at[index])
        for index in range(count)
    ]
    for copy in copies:
        copy.start()
    for copy in copies:
        copy.wait()


def per_device(
    features,
    self_weight,
    neigh_weight,
    out_bias,
    tile_masks,
    tile_live,
    tile_columns,
    node_degree,
    cotangent,
):
    rows_n = lax.axis_size("row")
    reps_n = lax.axis_size("rep")
    panel_rows, width = features.shape
    share = node_degree.shape[0]
    slots = tile_masks.shape[1]
    tile = tile_masks.shape[2]
    chips = reps_n // 2
    lanes = width // 2
    tile_rows = 2 * width // rows_n // (reps_n // 2)
    scale = 1.0 / math.sqrt(share * rows_n * reps_n)
    block = (share, width)
    anywhere = pl.BlockSpec(memory_space=pl.ANY)
    dma = pltpu.SemaphoreType.DMA
    vmem = pltpu.VMEM
    grads = (reps_n + 2, tile_rows, lanes)
    half_block = (share, lanes)
    turned = (lanes, share)
    scratch = [
        pltpu.SMEM((slots, panel_rows // tile), jnp.int32),
        pltpu.SMEM((slots, panel_rows // tile), jnp.int32),
        vmem((panel_rows, slots * share), BF),
        vmem((BUFFERS, tile * slots, tile), jnp.int32),
        vmem((2, *block), BF),
        vmem((2, rows_n * share, lanes), BF),
        vmem((width, width), BF),
        vmem((width, width), BF),
        vmem((1, width), F32),
        vmem((1, share), jnp.int32),
        vmem(block, BF),
        vmem((4, 2, *half_block), F32),
        vmem((2, chips, *half_block), BF),
        vmem((2, chips, *half_block), BF),
        vmem((2, chips, *half_block), BF),
        vmem((2, chips, *half_block), BF),
        vmem((2, *half_block), F32),
        vmem(block, F32),
        vmem(block, BF),
        vmem((2, lanes, panel_rows), BF),
        vmem((2, *turned), F32),
        vmem((2, *turned), F32),
        vmem((2, rows_n, *turned), BF),
        vmem((2, rows_n, *turned), BF),
        vmem((rows_n, *grads), F32),
        vmem((rows_n, *grads), F32),
        vmem(grads, F32),
        vmem((reps_n, 3, tile_rows, lanes), F32),
        vmem((reps_n, 3, tile_rows, lanes), F32),
        vmem((rows_n, tile_rows, lanes), F32),
        vmem((reps_n, rows_n, tile_rows, lanes), F32),
        dma((BUFFERS,)),
        dma((9,)),
        dma((2, rows_n)),
        dma((2, rows_n)),
    ]
    scratch += [dma((2, chips))] * 8 + [dma((2, rows_n))] * 2 + [dma((rows_n,))] * 2
    scratch += [dma((reps_n,))] * 2 + [dma((rows_n,))] * 2 + [dma((chips,))] * 4
    results = pl.pallas_call(
        functools.partial(kernel, rows_n, reps_n, scale),
        out_shape=(
            vmem(block, BF),
            vmem(block, BF),
            vmem((width, width), F32),
            vmem((width, width), F32),
            vmem((1, width), F32),
        ),
        in_specs=[anywhere] * 9,
        out_specs=(pl.BlockSpec(memory_space=vmem),) * 5,
        scratch_shapes=scratch,
        compiler_params=pltpu.CompilerParams(
            collective_id=0, has_side_effects=True, vmem_limit_bytes=56 * 1024 * 1024
        ),
        name="layer",
    )(
        features,
        self_weight,
        neigh_weight,
        out_bias.reshape(1, width),
        tile_masks.reshape(panel_rows * slots, tile),
        tile_live.T,
        tile_columns.T,
        node_degree.reshape(1, share),
        cotangent,
    )
    hidden, grad_features, grad_self, grad_neigh, grad_bias = pl.pallas_call(
        store,
        out_shape=tuple(jax.ShapeDtypeStruct(one.shape, one.dtype) for one in results),
        in_specs=[pl.BlockSpec(memory_space=vmem)] * 5,
        out_specs=(anywhere,) * 5,
        scratch_shapes=[dma((5,))],
        name="store",
    )(*[pltpu.with_memory_space_constraint(one, vmem) for one in results])
    return (hidden, grad_features, grad_self, grad_neigh, grad_bias.reshape(width))


def solution(mesh):
    return jax.shard_map(
        per_device,
        mesh=mesh,
        in_specs=(
            P("row", None),
            P(),
            P(),
            P(),
            P("row", "rep", None),
            P("row", "rep"),
            P("row", "rep"),
            P(("row", "rep")),
            P(("row", "rep"), None),
        ),
        out_specs=(P(("row", "rep"), None), P(("row", "rep"), None), P(), P(), P()),
        check_vma=False,
    )
```

```python
import functools
import math

import jax
import jax.numpy as jnp
from jax import lax
from jax.experimental import pallas as pl
from jax.experimental.pallas import tpu as pltpu
from jax.sharding import PartitionSpec as P

BF = jnp.bfloat16
F32 = jnp.float32
BUFFERS = 16
LAG = 2
CONTRACT_LAST = (((1,), (1,)), ((), ()))
CONTRACT_FIRST = (((0,), (0,)), ((), ()))


def kernel(
    rows_n,
    reps_n,
    scale,
    features,
    self_weight,
    neigh_weight,
    bias,
    masks,
    live_hbm,
    column_hbm,
    degree,
    cotangent,
    hid_v,
    gf_v,
    gs_v,
    gn_v,
    gb_v,
    live,
    column,
    dense,
    mask_buf,
    feat_v,
    gathered,
    sw_v,
    nw_v,
    bias_v,
    degree_v,
    cot_v,
    work,
    pair_send,
    pair_recv,
    part_send,
    part_recv,
    own_sum,
    pre_v,
    mean_v,
    msg_all,
    direct,
    back_own,
    back_send,
    back_recv,
    g_term,
    g_pair,
    g1_send,
    g1_recv,
    g1_sum,
    g2_send,
    g2_recv,
    g3,
    g4,
    mask_sem,
    in_sem,
    s1,
    r1,
    s2p,
    r2p,
    s2,
    r2,
    s3,
    r3,
    s3f,
    r3f,
    s4,
    r4,
    sg0,
    rg0,
    sg1,
    rg1,
    sg2,
    rg2,
    sg3,
    rg3,
    sg4,
    rg4,
    sg4f,
    rg4f,
):
    width = self_weight.shape[0]
    share = cotangent.shape[0]
    half = width // 2
    tile = masks.shape[1]
    half_rows = rows_n // 2
    chips = reps_n // 2
    ring = chips // 2
    mask_rows = tile * rows_n
    blocks = masks.shape[0] // mask_rows
    slot_width = share
    row = lax.axis_index("row")
    rep = lax.axis_index("rep")
    core = lax.rem(rep, 2)
    chip = lax.div(rep, 2)
    row_far, row_step = lax.div(row, half_rows), lax.rem(row, half_rows)
    chip_across, chip_along = lax.div(chip, ring), lax.rem(chip, ring)
    sibling = chip * 2 + 1 - core
    far_rep = lax.rem(rep + reps_n // 2, reps_n)

    def remote(src, dst, send, recv, to_row, to_rep):
        return pltpu.make_async_remote_copy(
            src_ref=src,
            dst_ref=dst,
            send_sem=send,
            recv_sem=recv,
            device_id=(to_row, to_rep),
            device_id_type=pl.DeviceIdType.MESH,
        )

    def share_rows(index):
        return pl.ds(pl.multiple_of(index * share, share), share)

    def row_at(far, step):
        return lax.rem(row_far + far, 2) * half_rows + lax.rem(row_step + step, half_rows)

    def chip_at(across, along):
        return lax.rem(chip_across + across, 2) * ring + lax.rem(chip_along + along, ring)

    def chip_from(across, along):
        return lax.rem(chip_across + across, 2) * ring + lax.rem(chip_along + ring - along, ring)

    def offset(t, size):
        if isinstance(t, int):
            across, turn = (t + 1) % 2, t // 2
            return across, (1 + turn if across else size - 1 - turn) % size
        across, turn = lax.rem(t + 1, 2), lax.div(t, 2)
        return across, lax.rem(across * (1 + turn) + (1 - across) * (size - 1 - turn), size)

    row_steps = [
        (far, step) for step in range(half_rows) for far in range(2) if (far, step) != (0, 0)
    ]

    def mask_copy(block, slot):
        return pltpu.make_async_copy(
            masks.at[pl.ds(pl.multiple_of(block * mask_rows, mask_rows), mask_rows), :],
            mask_buf.at[slot],
            mask_sem.at[slot],
        )

    def greet(to_row, to_rep):
        pl.semaphore_signal(
            barrier, inc=1, device_id=(to_row, to_rep), device_id_type=pl.DeviceIdType.MESH
        )

    barrier = pltpu.get_barrier_semaphore()
    greeted = 0
    for far, step in row_steps:
        greet(row_at(far, step), rep)
        greeted += 1
        if far:
            greet(row_at(far, step), far_rep)
            greeted += 1
    for step in range(1, reps_n):
        greet(row, lax.rem(rep + step, reps_n))
        greeted += 1

    inputs = [
        pltpu.make_async_copy(src, dst, in_sem.at[index])
        for index, (src, dst) in enumerate(
            (
                (features.at[share_rows(rep), :], feat_v.at[0]),
                (features.at[share_rows(far_rep), :], feat_v.at[1]),
                (live_hbm, live),
                (column_hbm, column),
                (self_weight, sw_v),
                (neigh_weight, nw_v),
                (bias, bias_v),
                (degree, degree_v),
                (cotangent, cot_v),
            )
        )
    ]
    for copy in inputs[:4]:
        copy.start()

    def expand(block, carry):
        slot = lax.rem(block, BUFFERS)
        mask_copy(block, slot).wait()
        at = pl.ds(pl.multiple_of(block * tile, tile), tile)
        for s in range(rows_n):
            bits = mask_buf[slot, pl.ds(s, tile, stride=rows_n), :].astype(F32)
            held = live[s, block].astype(F32)
            second = held * column[s, block].astype(F32)
            first = held - second
            dense[at, s * slot_width : s * slot_width + tile] = (bits * first).astype(BF)
            dense[at, s * slot_width + tile : (s + 1) * slot_width] = (bits * second).astype(BF)

        @pl.when(block + BUFFERS < blocks)
        def _():
            mask_copy(block + BUFFERS, slot).start()

        return carry

    def feature_copy(part, far, step):
        return remote(
            feat_v.at[far, :, part * half : (part + 1) * half],
            gathered.at[part, share_rows(row), :],
            s1.at[part, far * half_rows + step],
            r1.at[part, far * half_rows + step],
            row_at(far, step),
            far_rep if far else rep,
        )

    for copy in inputs[:4]:
        copy.wait()
    pl.semaphore_wait(barrier, greeted)
    for far, step in row_steps:
        feature_copy(0, far, step).start()
    for block in range(BUFFERS):
        mask_copy(block, block).start()
    for copy in inputs[4:]:
        copy.start()
    early = blocks - blocks // 5
    lax.fori_loop(0, early, expand, 0)
    for far, step in row_steps:
        feature_copy(0, far, step).wait_send()
    for far, step in row_steps:
        feature_copy(1, far, step).start()
    lax.fori_loop(early, blocks, expand, 0)
    for copy in inputs[4:]:
        copy.wait()
    for part in range(2):
        gathered[part, share_rows(row), :] = feat_v[0, :, part * half : (part + 1) * half]
    own = feat_v[0]
    pre_v[...] = jnp.dot(own, sw_v[...], preferred_element_type=F32) + bias_v[...]
    degree_row = degree_v[...].astype(F32)
    degree_column = jnp.transpose(jnp.broadcast_to(degree_row, (half, share)))

    def pair_copy(part, t):
        return remote(
            pair_send.at[part, t],
            pair_recv.at[part, t],
            s2p.at[part, t],
            r2p.at[part, t],
            row,
            sibling,
        )

    def part_copy(part, t):
        return remote(
            part_send.at[part, t],
            part_recv.at[part, t],
            s2.at[part, t],
            r2.at[part, t],
            row,
            chip_at(*offset(t, ring)) * 2 + core,
        )

    def finish_pair(part, t):
        pair_copy(part, t).wait_recv()
        part_send[part, t] = (work[t % 4 if isinstance(t, int) else lax.rem(t, 4), core] + pair_recv[part, t].astype(F32)).astype(BF)
        part_copy(part, t).start()

    def forward(part):
        def body(t, carry):
            at = chip_at(*offset(t, ring))
            rows = pl.ds(pl.multiple_of(at * (2 * share), 2 * share), 2 * share)
            work[lax.rem(t, 4)] = jnp.dot(
                dense[rows, :], gathered[part], preferred_element_type=F32
            ).reshape(2, share, half)
            pair_send[part, t] = work[lax.rem(t, 4), 1 - core].astype(BF)
            pair_copy(part, t).start()

            @pl.when(t >= LAG)
            def _():
                finish_pair(part, t - LAG)

            return carry

        for far, step in row_steps:
            feature_copy(part, far, step).wait_recv()
        lax.fori_loop(0, chips, body, 0)
        for t in range(max(chips - LAG, 0), chips - 1):
            finish_pair(part, t)
        pair_copy(part, chips - 1).wait_recv()
        own_sum[part] = work[(chips - 1) % 4, core] + pair_recv[part, chips - 1].astype(F32)

    forward(0)
    forward(1)
    for part in range(2):
        total = own_sum[part]
        for t in range(chips - 1):
            part_copy(part, t).wait_recv()
            total = total + part_recv[part, t].astype(F32)
        mean = (total / degree_column).astype(BF)
        mean_v[:, part * half : (part + 1) * half] = mean
        pre_v[...] += jnp.dot(
            mean, nw_v[part * half : (part + 1) * half, :], preferred_element_type=F32
        )

    pre = pre_v[...]
    root = math.sqrt(2.0 / math.pi)
    square = pre * pre
    bend = jnp.tanh(root * (pre + 0.044715 * (square * pre)))
    slope = 0.5 * (1.0 + bend) + (0.5 * root) * pre * (1.0 - bend * bend) * (
        1.0 + (3.0 * 0.044715) * square
    )
    dpre = cot_v[...].astype(F32) * slope
    dpre_b = dpre.astype(BF)

    def message_copy(part, across, along):
        relay = relayed(part, across, along)
        source = (chip_at(1, 0) if relay else chip) * 2 + core
        place = msg_all.at[part, :, share_rows(source)]
        index = across * ring + along
        target = chip_at(0 if relay else across, along) * 2 + core
        return remote(place, place, s3.at[part, index], r3.at[part, index], row, target)

    def sibling_copy(part, across, along):
        place = msg_all.at[part, :, share_rows(chip_from(across, along) * 2 + core)]
        index = across * ring + along
        return remote(place, place, s3f.at[part, index], r3f.at[part, index], row, sibling)

    along_order = sorted(range(1, ring), key=lambda d: min(d, ring - d))

    def relayed(part, across, along):
        return across == 1 and along > 0 and (part == 1 or along == ring // 2)

    own_first = [(1, 0)] + [
        (across, along)
        for along in along_order
        for across in range(2)
        if not relayed(0, across, along)
    ]
    relay_first = [(1, along) for along in along_order if relayed(0, 1, along)]
    all_second = [(across, along) for along in along_order for across in range(2)]

    def finish_messages(part):
        for across in range(2):
            for along in along_order:
                message_copy(part, across, along).wait_recv()
                sibling_copy(part, across, along).start()
        for across in range(2):
            for along in range(ring):
                sibling_copy(part, across, along).wait_recv()

    for part in range(2):
        msg_all[part, :, share_rows(rep)] = (
            lax.dot_general(
                nw_v[part * half : (part + 1) * half, :],
                dpre_b,
                CONTRACT_LAST,
                preferred_element_type=F32,
            )
            / degree_row
        ).astype(BF)
        if part == 0:
            for offsets in own_first:
                message_copy(0, *offsets).start()
            sibling_copy(0, 0, 0).start()
        else:
            message_copy(1, 1, 0).start()
            sibling_copy(1, 0, 0).start()

    hid_v[...] = (0.5 * pre * (1.0 + bend)).astype(BF)

    g_rows = width // rows_n
    tile_rows = g_rows // (chips // 2)
    bias_term = jnp.broadcast_to(jnp.sum(dpre, axis=0, keepdims=True) * scale, (8, width))
    for index, left in enumerate((feat_v[0], mean_v[...])):
        g_term[index, :width, :] = (
            lax.dot_general(left, dpre_b, CONTRACT_FIRST, preferred_element_type=F32) * scale
        )
        g_term[index, width:, :] = bias_term

    def g0_copy():
        return remote(g_term.at[1 - core], g_pair, sg0.at[0], rg0.at[0], row, sibling)

    g0_copy().start()
    direct[...] = lax.dot_general(
        sw_v[...], dpre_b, CONTRACT_LAST, preferred_element_type=F32
    ).reshape(2, half, share)

    def g1_copy(far, step):
        index = far * half_rows + step
        to_row = row_at(far, step)
        return remote(
            g1_send.at[to_row],
            g1_recv.at[index],
            sg1.at[index],
            rg1.at[index],
            to_row,
            far_rep if far else rep,
        )

    def back_copy(part, t):
        return remote(
            back_send.at[part, t],
            back_recv.at[part, t],
            s4.at[part, t],
            r4.at[part, t],
            row_at(*offset(t, half_rows)),
            rep,
        )

    def backward(part, low, high):
        def body(t, carry):
            target = row_at(*offset(t, half_rows))
            columns = pl.ds(pl.multiple_of(target * slot_width, slot_width), slot_width)
            term = jnp.dot(msg_all[part], dense[:, columns], preferred_element_type=F32)

            @pl.when(t < rows_n - 1)
            def _():
                back_send[part, t] = term.astype(BF)
                back_copy(part, t).start()

            @pl.when(t == rows_n - 1)
            def _():
                back_own[part] = term

            return carry

        lax.fori_loop(low, high, body, 0)

    message_copy(0, 1, 0).wait_recv()
    for offsets in relay_first:
        message_copy(0, *offsets).start()
    sibling_copy(0, 1, 0).start()
    g0_copy().wait_recv()
    summed = g_term[core] + g_pair[...]
    for index in range(rows_n):
        for side in range(2):
            g1_send[index, side * (chips // 2) : (side + 1) * (chips // 2)] = summed[
                index * g_rows : (index + 1) * g_rows, side * half : (side + 1) * half
            ].reshape(chips // 2, tile_rows, half)
            g1_send[index, chips + side] = jnp.broadcast_to(
                summed[width : width + 1, side * half : (side + 1) * half], (tile_rows, half)
            )
    for far, step in row_steps:
        g1_copy(far, step).start()
    for offsets in own_first:
        message_copy(0, *offsets).wait_send()
    message_copy(1, 1, 0).wait_recv()
    for offsets in all_second:
        message_copy(1, *offsets).start()
    sibling_copy(1, 1, 0).start()
    finish_messages(0)
    def g2_copy(t):
        to_chip = chip_at(*offset(t, ring))
        return remote(
            g2_send.at[to_chip], g2_recv.at[t], sg2.at[t], rg2.at[t], row, to_chip * 2 + core
        )

    def g3_copy(far, step):
        index = far * half_rows + step
        return remote(g3.at[row], g3.at[row], sg3.at[index], rg3.at[index], row_at(far, step), rep)

    def g4_copy(t):
        to_rep = chip_at(*offset(t, ring)) * 2 + core
        return remote(g3, g4.at[core, chip], sg4.at[t], rg4.at[t], row, to_rep)

    def g4_pair(t):
        place = g4.at[core, chip_from(*offset(t, ring))]
        return remote(place, place, sg4f.at[t], rg4f.at[t], row, sibling)

    total = g1_send[row]
    for far, step in row_steps:
        g1_copy(far, step).wait_recv()
        total = total + g1_recv[far * half_rows + step]
    g1_sum[...] = total
    for index in range(chips):
        g2_send[index, 0] = g1_sum[index]
        g2_send[index, 1] = g1_sum[chips]
        g2_send[index, 2] = g1_sum[chips + 1]
    for t in range(chips - 1):
        g2_copy(t).start()
    backward(0, 0, rows_n)
    total = g2_send[chip]
    for t in range(chips - 1):
        g2_copy(t).wait_recv()
        total = total + g2_recv[t]
    g3[row] = total[0]
    for far, step in row_steps:
        g3_copy(far, step).start()
    for side in range(2):
        gb_v[:, side * half : (side + 1) * half] = total[1 + side][0:1, :]
    finish_messages(1)
    backward(1, 0, rows_n // 2)
    for far, step in row_steps:
        g3_copy(far, step).wait_recv()
    for t in range(chips - 1):
        g4_copy(t).start()
    g4[core, chip] = g3[...]
    g4_pair(chips - 1).start()
    backward(1, rows_n // 2, rows_n)

    def column_sums(part):
        total = direct[part] + back_own[part]
        for t in range(rows_n - 1):
            back_copy(part, t).wait_recv()
            total = total + back_recv[part, t].astype(F32)
        gf_v[:, part * half : (part + 1) * half] = jnp.transpose(total).astype(BF)

    column_sums(0)
    for t in range(chips - 1):
        g4_copy(t).wait_recv()
        g4_pair(t).start()
    for t in range(chips):
        g4_pair(t).wait_recv()
    for index, out in enumerate((gs_v, gn_v)):
        for place in range(rows_n):
            for side in range(2):
                out[
                    place * g_rows : (place + 1) * g_rows, side * half : (side + 1) * half
                ] = g4[index, side * (chips // 2) : (side + 1) * (chips // 2), place].reshape(
                    g_rows, half
                )
    column_sums(1)

    for far, step in row_steps:
        feature_copy(1, far, step).wait_send()
        g1_copy(far, step).wait_send()
        g3_copy(far, step).wait_send()
    for part in range(2):
        for t in range(chips):
            pair_copy(part, t).wait_send()
        for t in range(chips - 1):
            part_copy(part, t).wait_send()
        for t in range(rows_n - 1):
            back_copy(part, t).wait_send()
        for across in range(2):
            for along in range(ring):
                if (across or along) and not (part == 0 and (across, along) in own_first):
                    message_copy(part, across, along).wait_send()
                sibling_copy(part, across, along).wait_send()
    g0_copy().wait_send()
    for t in range(chips):
        if t < chips - 1:
            g2_copy(t).wait_send()
            g4_copy(t).wait_send()
        g4_pair(t).wait_send()


def store(*refs):
    count = len(refs) // 2
    sems = refs[-1]
    copies = [
        pltpu.make_async_copy(refs[index], refs[count + index], sems.at[index])
        for index in range(count)
    ]
    for copy in copies:
        copy.start()
    for copy in copies:
        copy.wait()


def per_device(
    features,
    self_weight,
    neigh_weight,
    out_bias,
    tile_masks,
    tile_live,
    tile_columns,
    node_degree,
    cotangent,
):
    rows_n = lax.axis_size("row")
    reps_n = lax.axis_size("rep")
    panel_rows, width = features.shape
    share = node_degree.shape[0]
    slots = tile_masks.shape[1]
    tile = tile_masks.shape[2]
    chips = reps_n // 2
    lanes = width // 2
    tile_rows = width // rows_n // (chips // 2)
    scale = 1.0 / math.sqrt(share * rows_n * reps_n)
    block = (share, width)
    anywhere = pl.BlockSpec(memory_space=pl.ANY)
    dma = pltpu.SemaphoreType.DMA
    vmem = pltpu.VMEM
    grads = (chips + 2, tile_rows, lanes)
    half_block = (share, lanes)
    turned = (lanes, share)
    scratch = [
        pltpu.SMEM((slots, panel_rows // tile), jnp.int32),
        pltpu.SMEM((slots, panel_rows // tile), jnp.int32),
        vmem((panel_rows, slots * share), BF),
        vmem((BUFFERS, tile * slots, tile), jnp.int32),
        vmem((2, *block), BF),
        vmem((2, rows_n * share, lanes), BF),
        vmem((width, width), BF),
        vmem((width, width), BF),
        vmem((1, width), F32),
        vmem((1, share), jnp.int32),
        vmem(block, BF),
        vmem((4, 2, *half_block), F32),
        vmem((2, chips, *half_block), BF),
        vmem((2, chips, *half_block), BF),
        vmem((2, chips, *half_block), BF),
        vmem((2, chips, *half_block), BF),
        vmem((2, *half_block), F32),
        vmem(block, F32),
        vmem(block, BF),
        vmem((2, lanes, panel_rows), BF),
        vmem((2, *turned), F32),
        vmem((2, *turned), F32),
        vmem((2, rows_n, *turned), BF),
        vmem((2, rows_n, *turned), BF),
        vmem((2, width + 8, width), F32),
        vmem((width + 8, width), F32),
        vmem((rows_n, *grads), F32),
        vmem((rows_n, *grads), F32),
        vmem(grads, F32),
        vmem((chips, 3, tile_rows, lanes), F32),
        vmem((chips, 3, tile_rows, lanes), F32),
        vmem((rows_n, tile_rows, lanes), F32),
        vmem((2, chips, rows_n, tile_rows, lanes), F32),
        dma((BUFFERS,)),
        dma((9,)),
        dma((2, rows_n)),
        dma((2, rows_n)),
    ]
    scratch += [dma((2, chips))] * 8 + [dma((2, rows_n))] * 2 + [dma((1,))] * 2 + [dma((rows_n,))] * 2
    scratch += [dma((chips,))] * 2 + [dma((rows_n,))] * 2 + [dma((chips,))] * 4
    results = pl.pallas_call(
        functools.partial(kernel, rows_n, reps_n, scale),
        out_shape=(
            vmem(block, BF),
            vmem(block, BF),
            vmem((width, width), F32),
            vmem((width, width), F32),
            vmem((1, width), F32),
        ),
        in_specs=[anywhere] * 9,
        out_specs=(pl.BlockSpec(memory_space=vmem),) * 5,
        scratch_shapes=scratch,
        compiler_params=pltpu.CompilerParams(
            collective_id=0, has_side_effects=True, vmem_limit_bytes=56 * 1024 * 1024
        ),
        name="layer",
    )(
        features,
        self_weight,
        neigh_weight,
        out_bias.reshape(1, width),
        tile_masks.reshape(panel_rows * slots, tile),
        tile_live.T,
        tile_columns.T,
        node_degree.reshape(1, share),
        cotangent,
    )
    hidden, grad_features, grad_self, grad_neigh, grad_bias = pl.pallas_call(
        store,
        out_shape=tuple(jax.ShapeDtypeStruct(one.shape, one.dtype) for one in results),
        in_specs=[pl.BlockSpec(memory_space=vmem)] * 5,
        out_specs=(anywhere,) * 5,
        scratch_shapes=[dma((5,))],
        name="store",
    )(*[pltpu.with_memory_space_constraint(one, vmem) for one in results])
    return (hidden, grad_features, grad_self, grad_neigh, grad_bias.reshape(width))


def solution(mesh):
    return jax.shard_map(
        per_device,
        mesh=mesh,
        in_specs=(
            P("row", None),
            P(),
            P(),
            P(),
            P("row", "rep", None),
            P("row", "rep"),
            P("row", "rep"),
            P(("row", "rep")),
            P(("row", "rep"), None),
        ),
        out_specs=(P(("row", "rep"), None), P(("row", "rep"), None), P(), P(), P()),
        check_vma=False,
    )
```

```python
import functools
import math

import jax
import jax.numpy as jnp
from jax import lax
from jax.experimental import pallas as pl
from jax.experimental.pallas import tpu as pltpu
from jax.sharding import PartitionSpec as P

BF = jnp.bfloat16
F32 = jnp.float32
BUFFERS = 16
LAG = 2
CONTRACT_LAST = (((1,), (1,)), ((), ()))
CONTRACT_FIRST = (((0,), (0,)), ((), ()))


def kernel(
    rows_n,
    reps_n,
    scale,
    features,
    self_weight,
    neigh_weight,
    bias,
    masks,
    live_hbm,
    column_hbm,
    degree,
    cotangent,
    hid_v,
    gf_v,
    gs_v,
    gn_v,
    gb_v,
    live,
    column,
    dense,
    mask_buf,
    feat_v,
    gathered,
    sw_v,
    nw_v,
    bias_v,
    degree_v,
    cot_v,
    work,
    pair_send,
    pair_recv,
    part_send,
    part_recv,
    own_sum,
    pre_v,
    mean_v,
    msg_all,
    direct,
    back_own,
    back_send,
    back_recv,
    g_term,
    g_pair,
    g1_send,
    g1_recv,
    g1_sum,
    g2_send,
    g2_recv,
    g3,
    g4,
    mask_sem,
    in_sem,
    s1,
    r1,
    s2p,
    r2p,
    s2,
    r2,
    s3,
    r3,
    s3f,
    r3f,
    s4,
    r4,
    sg0,
    rg0,
    sg1,
    rg1,
    sg2,
    rg2,
    sg3,
    rg3,
    sg4,
    rg4,
    sg4f,
    rg4f,
):
    width = self_weight.shape[0]
    share = cotangent.shape[0]
    half = width // 2
    tile = masks.shape[1]
    half_rows = rows_n // 2
    chips = reps_n // 2
    ring = chips // 2
    mask_rows = tile * rows_n
    blocks = masks.shape[0] // mask_rows
    slot_width = share
    row = lax.axis_index("row")
    rep = lax.axis_index("rep")
    core = lax.rem(rep, 2)
    chip = lax.div(rep, 2)
    row_far, row_step = lax.div(row, half_rows), lax.rem(row, half_rows)
    chip_across, chip_along = lax.div(chip, ring), lax.rem(chip, ring)
    sibling = chip * 2 + 1 - core
    far_rep = lax.rem(rep + reps_n // 2, reps_n)

    def remote(src, dst, send, recv, to_row, to_rep):
        return pltpu.make_async_remote_copy(
            src_ref=src,
            dst_ref=dst,
            send_sem=send,
            recv_sem=recv,
            device_id=(to_row, to_rep),
            device_id_type=pl.DeviceIdType.MESH,
        )

    def share_rows(index):
        return pl.ds(pl.multiple_of(index * share, share), share)

    def row_at(far, step):
        return lax.rem(row_far + far, 2) * half_rows + lax.rem(row_step + step, half_rows)

    def chip_at(across, along):
        return lax.rem(chip_across + across, 2) * ring + lax.rem(chip_along + along, ring)

    def chip_from(across, along):
        return lax.rem(chip_across + across, 2) * ring + lax.rem(chip_along + ring - along, ring)

    def offset(t, size):
        if isinstance(t, int):
            across, turn = (t + 1) % 2, t // 2
            return across, (1 + turn if across else size - 1 - turn) % size
        across, turn = lax.rem(t + 1, 2), lax.div(t, 2)
        return across, lax.rem(across * (1 + turn) + (1 - across) * (size - 1 - turn), size)

    row_steps = sorted(
        ((far, step) for step in range(half_rows) for far in range(2) if (far, step) != (0, 0)),
        key=lambda at: (-min(at[1], half_rows - at[1]), -at[0]),
    )

    def mask_copy(block, slot):
        return pltpu.make_async_copy(
            masks.at[pl.ds(pl.multiple_of(block * mask_rows, mask_rows), mask_rows), :],
            mask_buf.at[slot],
            mask_sem.at[slot],
        )

    def greet(to_row, to_rep):
        pl.semaphore_signal(
            barrier, inc=1, device_id=(to_row, to_rep), device_id_type=pl.DeviceIdType.MESH
        )

    barrier = pltpu.get_barrier_semaphore()
    greeted = 0
    for far, step in row_steps:
        greet(row_at(far, step), rep)
        greeted += 1
        if far:
            greet(row_at(far, step), far_rep)
            greeted += 1
    for step in range(1, reps_n):
        greet(row, lax.rem(rep + step, reps_n))
        greeted += 1

    inputs = [
        pltpu.make_async_copy(src, dst, in_sem.at[index])
        for index, (src, dst) in enumerate(
            (
                (features.at[share_rows(rep), :], feat_v.at[0]),
                (features.at[share_rows(far_rep), :], feat_v.at[1]),
                (live_hbm, live),
                (column_hbm, column),
                (self_weight, sw_v),
                (neigh_weight, nw_v),
                (bias, bias_v),
                (degree, degree_v),
                (cotangent, cot_v),
            )
        )
    ]
    for copy in inputs[:4]:
        copy.start()

    def expand(block, carry):
        slot = lax.rem(block, BUFFERS)
        mask_copy(block, slot).wait()
        at = pl.ds(pl.multiple_of(block * tile, tile), tile)
        for s in range(rows_n):
            bits = mask_buf[slot, pl.ds(s, tile, stride=rows_n), :].astype(F32)
            held = live[s, block].astype(F32)
            second = held * column[s, block].astype(F32)
            first = held - second
            dense[at, s * slot_width : s * slot_width + tile] = (bits * first).astype(BF)
            dense[at, s * slot_width + tile : (s + 1) * slot_width] = (bits * second).astype(BF)

        @pl.when(block + BUFFERS < blocks)
        def _():
            mask_copy(block + BUFFERS, slot).start()

        return carry

    def feature_copy(part, far, step):
        return remote(
            feat_v.at[far, :, part * half : (part + 1) * half],
            gathered.at[part, share_rows(row), :],
            s1.at[part, far * half_rows + step],
            r1.at[part, far * half_rows + step],
            row_at(far, step),
            far_rep if far else rep,
        )

    for copy in inputs[:4]:
        copy.wait()
    pl.semaphore_wait(barrier, greeted)
    for far, step in row_steps:
        feature_copy(0, far, step).start()
    for block in range(BUFFERS):
        mask_copy(block, block).start()
    for copy in inputs[4:]:
        copy.start()
    early = blocks - blocks // 5
    lax.fori_loop(0, early, expand, 0)
    for far, step in row_steps:
        feature_copy(0, far, step).wait_send()
    for far, step in row_steps:
        feature_copy(1, far, step).start()
    lax.fori_loop(early, blocks, expand, 0)
    for copy in inputs[4:]:
        copy.wait()
    for part in range(2):
        gathered[part, share_rows(row), :] = feat_v[0, :, part * half : (part + 1) * half]
    own = feat_v[0]
    pre_v[...] = jnp.dot(own, sw_v[...], preferred_element_type=F32) + bias_v[...]
    degree_row = degree_v[...].astype(F32)
    degree_column = jnp.transpose(jnp.broadcast_to(degree_row, (half, share)))

    def pair_copy(part, t):
        return remote(
            pair_send.at[part, t],
            pair_recv.at[part, t],
            s2p.at[part, t],
            r2p.at[part, t],
            row,
            sibling,
        )

    def part_copy(part, t):
        return remote(
            part_send.at[part, t],
            part_recv.at[part, t],
            s2.at[part, t],
            r2.at[part, t],
            row,
            chip_at(*offset(t, ring)) * 2 + core,
        )

    def finish_pair(part, t):
        pair_copy(part, t).wait_recv()
        part_send[part, t] = (work[t % 4 if isinstance(t, int) else lax.rem(t, 4), core] + pair_recv[part, t].astype(F32)).astype(BF)
        part_copy(part, t).start()

    def forward(part):
        def body(t, carry):
            at = chip_at(*offset(t, ring))
            rows = pl.ds(pl.multiple_of(at * (2 * share), 2 * share), 2 * share)
            work[lax.rem(t, 4)] = jnp.dot(
                dense[rows, :], gathered[part], preferred_element_type=F32
            ).reshape(2, share, half)
            pair_send[part, t] = work[lax.rem(t, 4), 1 - core].astype(BF)
            pair_copy(part, t).start()

            @pl.when(t >= LAG)
            def _():
                finish_pair(part, t - LAG)

            return carry

        for far, step in row_steps:
            feature_copy(part, far, step).wait_recv()
        lax.fori_loop(0, chips, body, 0)
        for t in range(max(chips - LAG, 0), chips - 1):
            finish_pair(part, t)
        pair_copy(part, chips - 1).wait_recv()
        own_sum[part] = work[(chips - 1) % 4, core] + pair_recv[part, chips - 1].astype(F32)

    forward(0)
    forward(1)
    for part in range(2):
        total = own_sum[part]
        for t in range(chips - 1):
            part_copy(part, t).wait_recv()
            total = total + part_recv[part, t].astype(F32)
        mean = (total / degree_column).astype(BF)
        mean_v[:, part * half : (part + 1) * half] = mean
        pre_v[...] += jnp.dot(
            mean, nw_v[part * half : (part + 1) * half, :], preferred_element_type=F32
        )

    pre = pre_v[...]
    root = math.sqrt(2.0 / math.pi)
    square = pre * pre
    bend = jnp.tanh(root * (pre + 0.044715 * (square * pre)))
    slope = 0.5 * (1.0 + bend) + (0.5 * root) * pre * (1.0 - bend * bend) * (
        1.0 + (3.0 * 0.044715) * square
    )
    dpre = cot_v[...].astype(F32) * slope
    dpre_b = dpre.astype(BF)

    def message_copy(part, across, along):
        relay = relayed(part, across, along)
        source = (chip_at(1, 0) if relay else chip) * 2 + core
        place = msg_all.at[part, :, share_rows(source)]
        index = across * ring + along
        target = chip_at(0 if relay else across, along) * 2 + core
        return remote(place, place, s3.at[part, index], r3.at[part, index], row, target)

    def sibling_copy(part, across, along):
        place = msg_all.at[part, :, share_rows(chip_from(across, along) * 2 + core)]
        index = across * ring + along
        return remote(place, place, s3f.at[part, index], r3f.at[part, index], row, sibling)

    along_order = sorted(range(1, ring), key=lambda d: min(d, ring - d))

    def relayed(part, across, along):
        return across == 1 and along > 0 and (part == 1 or along == ring // 2)

    own_first = [(1, 0)] + [
        (across, along)
        for along in along_order
        for across in range(2)
        if not relayed(0, across, along)
    ]
    relay_first = [(1, along) for along in along_order if relayed(0, 1, along)]
    all_second = [(across, along) for along in along_order for across in range(2)]

    def finish_messages(part):
        for across in range(2):
            for along in along_order:
                message_copy(part, across, along).wait_recv()
                sibling_copy(part, across, along).start()
        for across in range(2):
            for along in range(ring):
                sibling_copy(part, across, along).wait_recv()

    for part in range(2):
        msg_all[part, :, share_rows(rep)] = (
            lax.dot_general(
                nw_v[part * half : (part + 1) * half, :],
                dpre_b,
                CONTRACT_LAST,
                preferred_element_type=F32,
            )
            / degree_row
        ).astype(BF)
        if part == 0:
            for offsets in own_first:
                message_copy(0, *offsets).start()
            sibling_copy(0, 0, 0).start()
        else:
            message_copy(1, 1, 0).start()
            sibling_copy(1, 0, 0).start()

    hid_v[...] = (0.5 * pre * (1.0 + bend)).astype(BF)

    g_rows = width // rows_n
    tile_rows = g_rows // (chips // 2)
    bias_term = jnp.broadcast_to(jnp.sum(dpre, axis=0, keepdims=True) * scale, (8, width))
    for index, left in enumerate((feat_v[0], mean_v[...])):
        g_term[index, :width, :] = (
            lax.dot_general(left, dpre_b, CONTRACT_FIRST, preferred_element_type=F32) * scale
        )
        g_term[index, width:, :] = bias_term

    def g0_copy():
        return remote(g_term.at[1 - core], g_pair, sg0.at[0], rg0.at[0], row, sibling)

    g0_copy().start()
    direct[...] = lax.dot_general(
        sw_v[...], dpre_b, CONTRACT_LAST, preferred_element_type=F32
    ).reshape(2, half, share)

    def g1_copy(far, step):
        index = far * half_rows + step
        to_row = row_at(far, step)
        return remote(
            g1_send.at[to_row],
            g1_recv.at[index],
            sg1.at[index],
            rg1.at[index],
            to_row,
            far_rep if far else rep,
        )

    def back_copy(part, t):
        return remote(
            back_send.at[part, t],
            back_recv.at[part, t],
            s4.at[part, t],
            r4.at[part, t],
            row_at(*offset(t, half_rows)),
            rep,
        )

    def backward(part, low, high):
        def body(t, carry):
            target = row_at(*offset(t, half_rows))
            columns = pl.ds(pl.multiple_of(target * slot_width, slot_width), slot_width)
            term = jnp.dot(msg_all[part], dense[:, columns], preferred_element_type=F32)

            @pl.when(t < rows_n - 1)
            def _():
                back_send[part, t] = term.astype(BF)
                back_copy(part, t).start()

            @pl.when(t == rows_n - 1)
            def _():
                back_own[part] = term

            return carry

        lax.fori_loop(low, high, body, 0)

    message_copy(0, 1, 0).wait_recv()
    for offsets in relay_first:
        message_copy(0, *offsets).start()
    sibling_copy(0, 1, 0).start()
    g0_copy().wait_recv()
    summed = g_term[core] + g_pair[...]
    for index in range(rows_n):
        for side in range(2):
            g1_send[index, side * (chips // 2) : (side + 1) * (chips // 2)] = summed[
                index * g_rows : (index + 1) * g_rows, side * half : (side + 1) * half
            ].reshape(chips // 2, tile_rows, half)
            g1_send[index, chips + side] = jnp.broadcast_to(
                summed[width : width + 1, side * half : (side + 1) * half], (tile_rows, half)
            )
    for far, step in row_steps:
        g1_copy(far, step).start()
    for offsets in own_first:
        message_copy(0, *offsets).wait_send()
    message_copy(1, 1, 0).wait_recv()
    for offsets in all_second:
        message_copy(1, *offsets).start()
    sibling_copy(1, 1, 0).start()
    finish_messages(0)
    def g2_copy(t):
        to_chip = chip_at(*offset(t, ring))
        return remote(
            g2_send.at[to_chip], g2_recv.at[t], sg2.at[t], rg2.at[t], row, to_chip * 2 + core
        )

    def g3_copy(far, step):
        index = far * half_rows + step
        return remote(g3.at[row], g3.at[row], sg3.at[index], rg3.at[index], row_at(far, step), rep)

    def g4_copy(t):
        to_rep = chip_at(*offset(t, ring)) * 2 + core
        return remote(g3, g4.at[core, chip], sg4.at[t], rg4.at[t], row, to_rep)

    def g4_pair(t):
        place = g4.at[core, chip_from(*offset(t, ring))]
        return remote(place, place, sg4f.at[t], rg4f.at[t], row, sibling)

    total = g1_send[row]
    for far, step in row_steps:
        g1_copy(far, step).wait_recv()
        total = total + g1_recv[far * half_rows + step]
    g1_sum[...] = total
    for index in range(chips):
        g2_send[index, 0] = g1_sum[index]
        g2_send[index, 1] = g1_sum[chips]
        g2_send[index, 2] = g1_sum[chips + 1]
    for t in range(chips - 1):
        g2_copy(t).start()
    backward(0, 0, rows_n)
    total = g2_send[chip]
    for t in range(chips - 1):
        g2_copy(t).wait_recv()
        total = total + g2_recv[t]
    g3[row] = total[0]
    for far, step in row_steps:
        g3_copy(far, step).start()
    for side in range(2):
        gb_v[:, side * half : (side + 1) * half] = total[1 + side][0:1, :]
    finish_messages(1)
    backward(1, 0, rows_n // 2)
    for far, step in row_steps:
        g3_copy(far, step).wait_recv()
    for t in range(chips - 1):
        g4_copy(t).start()
    g4[core, chip] = g3[...]
    g4_pair(chips - 1).start()
    backward(1, rows_n // 2, rows_n)

    def column_sums(part):
        total = direct[part] + back_own[part]
        for t in range(rows_n - 1):
            back_copy(part, t).wait_recv()
            total = total + back_recv[part, t].astype(F32)
        gf_v[:, part * half : (part + 1) * half] = jnp.transpose(total).astype(BF)

    column_sums(0)
    for t in range(chips - 1):
        g4_copy(t).wait_recv()
        g4_pair(t).start()
    for t in range(chips):
        g4_pair(t).wait_recv()
    for index, out in enumerate((gs_v, gn_v)):
        for place in range(rows_n):
            for side in range(2):
                out[
                    place * g_rows : (place + 1) * g_rows, side * half : (side + 1) * half
                ] = g4[index, side * (chips // 2) : (side + 1) * (chips // 2), place].reshape(
                    g_rows, half
                )
    column_sums(1)

    for far, step in row_steps:
        feature_copy(1, far, step).wait_send()
        g1_copy(far, step).wait_send()
        g3_copy(far, step).wait_send()
    for part in range(2):
        for t in range(chips):
            pair_copy(part, t).wait_send()
        for t in range(chips - 1):
            part_copy(part, t).wait_send()
        for t in range(rows_n - 1):
            back_copy(part, t).wait_send()
        for across in range(2):
            for along in range(ring):
                if (across or along) and not (part == 0 and (across, along) in own_first):
                    message_copy(part, across, along).wait_send()
                sibling_copy(part, across, along).wait_send()
    g0_copy().wait_send()
    for t in range(chips):
        if t < chips - 1:
            g2_copy(t).wait_send()
            g4_copy(t).wait_send()
        g4_pair(t).wait_send()


def store(*refs):
    count = len(refs) // 2
    sems = refs[-1]
    copies = [
        pltpu.make_async_copy(refs[index], refs[count + index], sems.at[index])
        for index in range(count)
    ]
    for copy in copies:
        copy.start()
    for copy in copies:
        copy.wait()


def per_device(
    features,
    self_weight,
    neigh_weight,
    out_bias,
    tile_masks,
    tile_live,
    tile_columns,
    node_degree,
    cotangent,
):
    rows_n = lax.axis_size("row")
    reps_n = lax.axis_size("rep")
    panel_rows, width = features.shape
    share = node_degree.shape[0]
    slots = tile_masks.shape[1]
    tile = tile_masks.shape[2]
    chips = reps_n // 2
    lanes = width // 2
    tile_rows = width // rows_n // (chips // 2)
    scale = 1.0 / math.sqrt(share * rows_n * reps_n)
    block = (share, width)
    anywhere = pl.BlockSpec(memory_space=pl.ANY)
    dma = pltpu.SemaphoreType.DMA
    vmem = pltpu.VMEM
    grads = (chips + 2, tile_rows, lanes)
    half_block = (share, lanes)
    turned = (lanes, share)
    scratch = [
        pltpu.SMEM((slots, panel_rows // tile), jnp.int32),
        pltpu.SMEM((slots, panel_rows // tile), jnp.int32),
        vmem((panel_rows, slots * share), BF),
        vmem((BUFFERS, tile * slots, tile), jnp.int32),
        vmem((2, *block), BF),
        vmem((2, rows_n * share, lanes), BF),
        vmem((width, width), BF),
        vmem((width, width), BF),
        vmem((1, width), F32),
        vmem((1, share), jnp.int32),
        vmem(block, BF),
        vmem((4, 2, *half_block), F32),
        vmem((2, chips, *half_block), BF),
        vmem((2, chips, *half_block), BF),
        vmem((2, chips, *half_block), BF),
        vmem((2, chips, *half_block), BF),
        vmem((2, *half_block), F32),
        vmem(block, F32),
        vmem(block, BF),
        vmem((2, lanes, panel_rows), BF),
        vmem((2, *turned), F32),
        vmem((2, *turned), F32),
        vmem((2, rows_n, *turned), BF),
        vmem((2, rows_n, *turned), BF),
        vmem((2, width + 8, width), F32),
        vmem((width + 8, width), F32),
        vmem((rows_n, *grads), F32),
        vmem((rows_n, *grads), F32),
        vmem(grads, F32),
        vmem((chips, 3, tile_rows, lanes), F32),
        vmem((chips, 3, tile_rows, lanes), F32),
        vmem((rows_n, tile_rows, lanes), F32),
        vmem((2, chips, rows_n, tile_rows, lanes), F32),
        dma((BUFFERS,)),
        dma((9,)),
        dma((2, rows_n)),
        dma((2, rows_n)),
    ]
    scratch += [dma((2, chips))] * 8 + [dma((2, rows_n))] * 2 + [dma((1,))] * 2 + [dma((rows_n,))] * 2
    scratch += [dma((chips,))] * 2 + [dma((rows_n,))] * 2 + [dma((chips,))] * 4
    results = pl.pallas_call(
        functools.partial(kernel, rows_n, reps_n, scale),
        out_shape=(
            vmem(block, BF),
            vmem(block, BF),
            vmem((width, width), F32),
            vmem((width, width), F32),
            vmem((1, width), F32),
        ),
        in_specs=[anywhere] * 9,
        out_specs=(pl.BlockSpec(memory_space=vmem),) * 5,
        scratch_shapes=scratch,
        compiler_params=pltpu.CompilerParams(
            collective_id=0, has_side_effects=True, vmem_limit_bytes=56 * 1024 * 1024
        ),
        name="layer",
    )(
        features,
        self_weight,
        neigh_weight,
        out_bias.reshape(1, width),
        tile_masks.reshape(panel_rows * slots, tile),
        tile_live.T,
        tile_columns.T,
        node_degree.reshape(1, share),
        cotangent,
    )
    hidden, grad_features, grad_self, grad_neigh, grad_bias = pl.pallas_call(
        store,
        out_shape=tuple(jax.ShapeDtypeStruct(one.shape, one.dtype) for one in results),
        in_specs=[pl.BlockSpec(memory_space=vmem)] * 5,
        out_specs=(anywhere,) * 5,
        scratch_shapes=[dma((5,))],
        name="store",
    )(*[pltpu.with_memory_space_constraint(one, vmem) for one in results])
    return (hidden, grad_features, grad_self, grad_neigh, grad_bias.reshape(width))


def solution(mesh):
    return jax.shard_map(
        per_device,
        mesh=mesh,
        in_specs=(
            P("row", None),
            P(),
            P(),
            P(),
            P("row", "rep", None),
            P("row", "rep"),
            P("row", "rep"),
            P(("row", "rep")),
            P(("row", "rep"), None),
        ),
        out_specs=(P(("row", "rep"), None), P(("row", "rep"), None), P(), P(), P()),
        check_vma=False,
    )
```

```python
import functools
import math

import jax
import jax.numpy as jnp
from jax import lax
from jax.experimental import pallas as pl
from jax.experimental.pallas import tpu as pltpu
from jax.sharding import PartitionSpec as P

BF = jnp.bfloat16
F32 = jnp.float32
BUFFERS = 16
LAG = 2
CONTRACT_LAST = (((1,), (1,)), ((), ()))
CONTRACT_FIRST = (((0,), (0,)), ((), ()))


def kernel(
    rows_n,
    reps_n,
    scale,
    features,
    self_weight,
    neigh_weight,
    bias,
    masks,
    live_hbm,
    column_hbm,
    degree,
    cotangent,
    hid_v,
    gf_v,
    gs_v,
    gn_v,
    gb_v,
    live,
    column,
    dense,
    mask_buf,
    feat_v,
    gathered,
    sw_v,
    nw_v,
    bias_v,
    degree_v,
    cot_v,
    work,
    pair_send,
    pair_recv,
    part_send,
    part_recv,
    own_sum,
    pre_v,
    mean_v,
    msg_all,
    direct,
    back_own,
    back_send,
    back_recv,
    g_term,
    g_pair,
    g1_send,
    g1_recv,
    g1_sum,
    g2_send,
    g2_recv,
    g3,
    g4,
    mask_sem,
    in_sem,
    s1,
    r1,
    s2p,
    r2p,
    s2,
    r2,
    s3,
    r3,
    s3f,
    r3f,
    s4,
    r4,
    sg0,
    rg0,
    sg1,
    rg1,
    sg2,
    rg2,
    sg3,
    rg3,
    sg4,
    rg4,
    sg4f,
    rg4f,
):
    width = self_weight.shape[0]
    share = cotangent.shape[0]
    half = width // 2
    tile = masks.shape[1]
    half_rows = rows_n // 2
    chips = reps_n // 2
    ring = chips // 2
    mask_rows = tile * rows_n
    blocks = masks.shape[0] // mask_rows
    slot_width = share
    row = lax.axis_index("row")
    rep = lax.axis_index("rep")
    core = lax.rem(rep, 2)
    chip = lax.div(rep, 2)
    row_far, row_step = lax.div(row, half_rows), lax.rem(row, half_rows)
    chip_across, chip_along = lax.div(chip, ring), lax.rem(chip, ring)
    sibling = chip * 2 + 1 - core
    far_rep = lax.rem(rep + reps_n // 2, reps_n)

    def remote(src, dst, send, recv, to_row, to_rep):
        return pltpu.make_async_remote_copy(
            src_ref=src,
            dst_ref=dst,
            send_sem=send,
            recv_sem=recv,
            device_id=(to_row, to_rep),
            device_id_type=pl.DeviceIdType.MESH,
        )

    def share_rows(index):
        return pl.ds(pl.multiple_of(index * share, share), share)

    def row_at(far, step):
        return lax.rem(row_far + far, 2) * half_rows + lax.rem(row_step + step, half_rows)

    def chip_at(across, along):
        return lax.rem(chip_across + across, 2) * ring + lax.rem(chip_along + along, ring)

    def chip_from(across, along):
        return lax.rem(chip_across + across, 2) * ring + lax.rem(chip_along + ring - along, ring)

    def offset(t, size):
        if isinstance(t, int):
            across, turn = (t + 1) % 2, t // 2
            return across, (1 + turn if across else size - 1 - turn) % size
        across, turn = lax.rem(t + 1, 2), lax.div(t, 2)
        return across, lax.rem(across * (1 + turn) + (1 - across) * (size - 1 - turn), size)

    row_steps = sorted(
        ((far, step) for step in range(half_rows) for far in range(2) if (far, step) != (0, 0)),
        key=lambda at: (-min(at[1], half_rows - at[1]), -at[0]),
    )

    def mask_copy(block, slot):
        return pltpu.make_async_copy(
            masks.at[pl.ds(pl.multiple_of(block * mask_rows, mask_rows), mask_rows), :],
            mask_buf.at[slot],
            mask_sem.at[slot],
        )

    def greet(to_row, to_rep):
        pl.semaphore_signal(
            barrier, inc=1, device_id=(to_row, to_rep), device_id_type=pl.DeviceIdType.MESH
        )

    barrier = pltpu.get_barrier_semaphore()
    greeted = 0
    for far, step in row_steps:
        greet(row_at(far, step), rep)
        greeted += 1
        if far:
            greet(row_at(far, step), far_rep)
            greeted += 1
    for step in range(1, reps_n):
        greet(row, lax.rem(rep + step, reps_n))
        greeted += 1

    inputs = [
        pltpu.make_async_copy(src, dst, in_sem.at[index])
        for index, (src, dst) in enumerate(
            (
                (features.at[share_rows(rep), :], feat_v.at[0]),
                (features.at[share_rows(far_rep), :], feat_v.at[1]),
                (live_hbm, live),
                (column_hbm, column),
                (self_weight, sw_v),
                (neigh_weight, nw_v),
                (bias, bias_v),
                (degree, degree_v),
                (cotangent, cot_v),
            )
        )
    ]
    for copy in inputs[:4]:
        copy.start()

    def expand(block, carry):
        slot = lax.rem(block, BUFFERS)
        mask_copy(block, slot).wait()
        at = pl.ds(pl.multiple_of(block * tile, tile), tile)
        for s in range(rows_n):
            bits = mask_buf[slot, pl.ds(s, tile, stride=rows_n), :].astype(F32)
            held = live[s, block].astype(F32)
            second = held * column[s, block].astype(F32)
            first = held - second
            dense[at, s * slot_width : s * slot_width + tile] = (bits * first).astype(BF)
            dense[at, s * slot_width + tile : (s + 1) * slot_width] = (bits * second).astype(BF)

        @pl.when(block + BUFFERS < blocks)
        def _():
            mask_copy(block + BUFFERS, slot).start()

        return carry

    def feature_copy(part, far, step):
        return remote(
            feat_v.at[far, :, part * half : (part + 1) * half],
            gathered.at[part, share_rows(row), :],
            s1.at[part, far * half_rows + step],
            r1.at[part, far * half_rows + step],
            row_at(far, step),
            far_rep if far else rep,
        )

    for copy in inputs[:4]:
        copy.wait()
    pl.semaphore_wait(barrier, greeted)
    for far, step in row_steps:
        feature_copy(0, far, step).start()
    for block in range(BUFFERS):
        mask_copy(block, block).start()
    for copy in inputs[4:]:
        copy.start()
    early = blocks - blocks // 5
    lax.fori_loop(0, early, expand, 0)
    for far, step in row_steps:
        feature_copy(0, far, step).wait_send()
    for far, step in row_steps:
        feature_copy(1, far, step).start()
    lax.fori_loop(early, blocks, expand, 0)
    for copy in inputs[4:]:
        copy.wait()
    for part in range(2):
        gathered[part, share_rows(row), :] = feat_v[0, :, part * half : (part + 1) * half]
    own = feat_v[0]
    pre_v[...] = jnp.dot(own, sw_v[...], preferred_element_type=F32) + bias_v[...]
    degree_row = degree_v[...].astype(F32)
    degree_column = jnp.transpose(jnp.broadcast_to(degree_row, (half, share)))

    def pair_copy(part, t):
        return remote(
            pair_send.at[part, t],
            pair_recv.at[part, t],
            s2p.at[part, t],
            r2p.at[part, t],
            row,
            sibling,
        )

    def part_copy(part, t):
        return remote(
            part_send.at[part, t],
            part_recv.at[part, t],
            s2.at[part, t],
            r2.at[part, t],
            row,
            chip_at(*offset(t, ring)) * 2 + core,
        )

    def finish_pair(part, t):
        pair_copy(part, t).wait_recv()
        part_send[part, t] = (work[t % 4 if isinstance(t, int) else lax.rem(t, 4), core] + pair_recv[part, t].astype(F32)).astype(BF)
        part_copy(part, t).start()

    def forward(part):
        def body(t, carry):
            at = chip_at(*offset(t, ring))
            rows = pl.ds(pl.multiple_of(at * (2 * share), 2 * share), 2 * share)
            work[lax.rem(t, 4)] = jnp.dot(
                dense[rows, :], gathered[part], preferred_element_type=F32
            ).reshape(2, share, half)
            pair_send[part, t] = work[lax.rem(t, 4), 1 - core].astype(BF)
            pair_copy(part, t).start()

            @pl.when(t >= LAG)
            def _():
                finish_pair(part, t - LAG)

            return carry

        for far, step in row_steps:
            feature_copy(part, far, step).wait_recv()
        lax.fori_loop(0, chips, body, 0)
        for t in range(max(chips - LAG, 0), chips - 1):
            finish_pair(part, t)
        pair_copy(part, chips - 1).wait_recv()
        own_sum[part] = work[(chips - 1) % 4, core] + pair_recv[part, chips - 1].astype(F32)

    forward(0)
    forward(1)
    for part in range(2):
        total = own_sum[part]
        for t in range(chips - 1):
            part_copy(part, t).wait_recv()
            total = total + part_recv[part, t].astype(F32)
        mean = (total / degree_column).astype(BF)
        mean_v[:, part * half : (part + 1) * half] = mean
        pre_v[...] += jnp.dot(
            mean, nw_v[part * half : (part + 1) * half, :], preferred_element_type=F32
        )

    pre = pre_v[...]
    root = math.sqrt(2.0 / math.pi)
    square = pre * pre
    bend = jnp.tanh(root * (pre + 0.044715 * (square * pre)))
    slope = 0.5 * (1.0 + bend) + (0.5 * root) * pre * (1.0 - bend * bend) * (
        1.0 + (3.0 * 0.044715) * square
    )
    dpre = cot_v[...].astype(F32) * slope
    dpre_b = dpre.astype(BF)

    def message_copy(part, across, along):
        relay = relayed(part, across, along)
        source = (chip_at(1, 0) if relay else chip) * 2 + core
        place = msg_all.at[part, :, share_rows(source)]
        index = across * ring + along
        target = chip_at(0 if relay else across, along) * 2 + core
        return remote(place, place, s3.at[part, index], r3.at[part, index], row, target)

    def sibling_copy(part, across, along):
        place = msg_all.at[part, :, share_rows(chip_from(across, along) * 2 + core)]
        index = across * ring + along
        return remote(place, place, s3f.at[part, index], r3f.at[part, index], row, sibling)

    along_order = sorted(range(1, ring), key=lambda d: min(d, ring - d))

    def relayed(part, across, along):
        return across == 1 and along > 0 and (part == 1 or along == ring // 2)

    own_first = [(1, 0)] + [
        (across, along)
        for along in along_order
        for across in range(2)
        if not relayed(0, across, along)
    ]
    own_first.sort(key=lambda at: -2 * (at == (1, 0)) - (at[0] + min(at[1], ring - at[1]) > 1))
    relay_first = [(1, along) for along in along_order if relayed(0, 1, along)]
    all_second = [(across, along) for along in along_order for across in range(2)]

    def finish_messages(part):
        for across in range(2):
            for along in along_order:
                message_copy(part, across, along).wait_recv()
                sibling_copy(part, across, along).start()
        for across in range(2):
            for along in range(ring):
                sibling_copy(part, across, along).wait_recv()

    for part in range(2):
        msg_all[part, :, share_rows(rep)] = (
            lax.dot_general(
                nw_v[part * half : (part + 1) * half, :],
                dpre_b,
                CONTRACT_LAST,
                preferred_element_type=F32,
            )
            / degree_row
        ).astype(BF)
        if part == 0:
            for offsets in own_first:
                message_copy(0, *offsets).start()
            sibling_copy(0, 0, 0).start()
        else:
            message_copy(1, 1, 0).start()
            sibling_copy(1, 0, 0).start()

    hid_v[...] = (0.5 * pre * (1.0 + bend)).astype(BF)

    g_rows = width // rows_n
    tile_rows = g_rows // (chips // 2)
    bias_term = jnp.broadcast_to(jnp.sum(dpre, axis=0, keepdims=True) * scale, (8, width))
    for index, left in enumerate((feat_v[0], mean_v[...])):
        g_term[index, :width, :] = (
            lax.dot_general(left, dpre_b, CONTRACT_FIRST, preferred_element_type=F32) * scale
        )
        g_term[index, width:, :] = bias_term

    def g0_copy():
        return remote(g_term.at[1 - core], g_pair, sg0.at[0], rg0.at[0], row, sibling)

    g0_copy().start()
    direct[...] = lax.dot_general(
        sw_v[...], dpre_b, CONTRACT_LAST, preferred_element_type=F32
    ).reshape(2, half, share)

    def g1_copy(far, step):
        index = far * half_rows + step
        to_row = row_at(far, step)
        return remote(
            g1_send.at[to_row],
            g1_recv.at[index],
            sg1.at[index],
            rg1.at[index],
            to_row,
            far_rep if far else rep,
        )

    def back_copy(part, t):
        return remote(
            back_send.at[part, t],
            back_recv.at[part, t],
            s4.at[part, t],
            r4.at[part, t],
            row_at(*offset(t, half_rows)),
            rep,
        )

    def backward(part, low, high):
        def body(t, carry):
            target = row_at(*offset(t, half_rows))
            columns = pl.ds(pl.multiple_of(target * slot_width, slot_width), slot_width)
            term = jnp.dot(msg_all[part], dense[:, columns], preferred_element_type=F32)

            @pl.when(t < rows_n - 1)
            def _():
                back_send[part, t] = term.astype(BF)
                back_copy(part, t).start()

            @pl.when(t == rows_n - 1)
            def _():
                back_own[part] = term

            return carry

        lax.fori_loop(low, high, body, 0)

    message_copy(0, 1, 0).wait_recv()
    for offsets in relay_first:
        message_copy(0, *offsets).start()
    sibling_copy(0, 1, 0).start()
    g0_copy().wait_recv()
    summed = g_term[core] + g_pair[...]
    for index in range(rows_n):
        for side in range(2):
            g1_send[index, side * (chips // 2) : (side + 1) * (chips // 2)] = summed[
                index * g_rows : (index + 1) * g_rows, side * half : (side + 1) * half
            ].reshape(chips // 2, tile_rows, half)
            g1_send[index, chips + side] = jnp.broadcast_to(
                summed[width : width + 1, side * half : (side + 1) * half], (tile_rows, half)
            )
    for far, step in row_steps:
        g1_copy(far, step).start()
    for offsets in own_first:
        message_copy(0, *offsets).wait_send()
    message_copy(1, 1, 0).wait_recv()
    for offsets in all_second:
        message_copy(1, *offsets).start()
    sibling_copy(1, 1, 0).start()
    finish_messages(0)
    def g2_copy(t):
        to_chip = chip_at(*offset(t, ring))
        return remote(
            g2_send.at[to_chip], g2_recv.at[t], sg2.at[t], rg2.at[t], row, to_chip * 2 + core
        )

    def g3_copy(far, step):
        index = far * half_rows + step
        return remote(g3.at[row], g3.at[row], sg3.at[index], rg3.at[index], row_at(far, step), rep)

    def g4_copy(t):
        to_rep = chip_at(*offset(t, ring)) * 2 + core
        return remote(g3, g4.at[core, chip], sg4.at[t], rg4.at[t], row, to_rep)

    def g4_pair(t):
        place = g4.at[core, chip_from(*offset(t, ring))]
        return remote(place, place, sg4f.at[t], rg4f.at[t], row, sibling)

    total = g1_send[row]
    for far, step in row_steps:
        g1_copy(far, step).wait_recv()
        total = total + g1_recv[far * half_rows + step]
    g1_sum[...] = total
    for index in range(chips):
        g2_send[index, 0] = g1_sum[index]
        g2_send[index, 1] = g1_sum[chips]
        g2_send[index, 2] = g1_sum[chips + 1]
    for t in range(chips - 1):
        g2_copy(t).start()
    backward(0, 0, rows_n)
    total = g2_send[chip]
    for t in range(chips - 1):
        g2_copy(t).wait_recv()
        total = total + g2_recv[t]
    g3[row] = total[0]
    for far, step in row_steps:
        g3_copy(far, step).start()
    for side in range(2):
        gb_v[:, side * half : (side + 1) * half] = total[1 + side][0:1, :]
    finish_messages(1)
    backward(1, 0, rows_n // 2)
    for far, step in row_steps:
        g3_copy(far, step).wait_recv()
    for t in range(chips - 1):
        g4_copy(t).start()
    g4[core, chip] = g3[...]
    g4_pair(chips - 1).start()
    backward(1, rows_n // 2, rows_n)

    def column_sums(part):
        total = direct[part] + back_own[part]
        for t in range(rows_n - 1):
            back_copy(part, t).wait_recv()
            total = total + back_recv[part, t].astype(F32)
        gf_v[:, part * half : (part + 1) * half] = jnp.transpose(total).astype(BF)

    column_sums(0)
    for t in range(chips - 1):
        g4_copy(t).wait_recv()
        g4_pair(t).start()
    for t in range(chips):
        g4_pair(t).wait_recv()
    for index, out in enumerate((gs_v, gn_v)):
        for place in range(rows_n):
            for side in range(2):
                out[
                    place * g_rows : (place + 1) * g_rows, side * half : (side + 1) * half
                ] = g4[index, side * (chips // 2) : (side + 1) * (chips // 2), place].reshape(
                    g_rows, half
                )
    column_sums(1)

    for far, step in row_steps:
        feature_copy(1, far, step).wait_send()
        g1_copy(far, step).wait_send()
        g3_copy(far, step).wait_send()
    for part in range(2):
        for t in range(chips):
            pair_copy(part, t).wait_send()
        for t in range(chips - 1):
            part_copy(part, t).wait_send()
        for t in range(rows_n - 1):
            back_copy(part, t).wait_send()
        for across in range(2):
            for along in range(ring):
                if (across or along) and not (part == 0 and (across, along) in own_first):
                    message_copy(part, across, along).wait_send()
                sibling_copy(part, across, along).wait_send()
    g0_copy().wait_send()
    for t in range(chips):
        if t < chips - 1:
            g2_copy(t).wait_send()
            g4_copy(t).wait_send()
        g4_pair(t).wait_send()


def store(*refs):
    count = len(refs) // 2
    sems = refs[-1]
    copies = [
        pltpu.make_async_copy(refs[index], refs[count + index], sems.at[index])
        for index in range(count)
    ]
    for copy in copies:
        copy.start()
    for copy in copies:
        copy.wait()


def per_device(
    features,
    self_weight,
    neigh_weight,
    out_bias,
    tile_masks,
    tile_live,
    tile_columns,
    node_degree,
    cotangent,
):
    rows_n = lax.axis_size("row")
    reps_n = lax.axis_size("rep")
    panel_rows, width = features.shape
    share = node_degree.shape[0]
    slots = tile_masks.shape[1]
    tile = tile_masks.shape[2]
    chips = reps_n // 2
    lanes = width // 2
    tile_rows = width // rows_n // (chips // 2)
    scale = 1.0 / math.sqrt(share * rows_n * reps_n)
    block = (share, width)
    anywhere = pl.BlockSpec(memory_space=pl.ANY)
    dma = pltpu.SemaphoreType.DMA
    vmem = pltpu.VMEM
    grads = (chips + 2, tile_rows, lanes)
    half_block = (share, lanes)
    turned = (lanes, share)
    scratch = [
        pltpu.SMEM((slots, panel_rows // tile), jnp.int32),
        pltpu.SMEM((slots, panel_rows // tile), jnp.int32),
        vmem((panel_rows, slots * share), BF),
        vmem((BUFFERS, tile * slots, tile), jnp.int32),
        vmem((2, *block), BF),
        vmem((2, rows_n * share, lanes), BF),
        vmem((width, width), BF),
        vmem((width, width), BF),
        vmem((1, width), F32),
        vmem((1, share), jnp.int32),
        vmem(block, BF),
        vmem((4, 2, *half_block), F32),
        vmem((2, chips, *half_block), BF),
        vmem((2, chips, *half_block), BF),
        vmem((2, chips, *half_block), BF),
        vmem((2, chips, *half_block), BF),
        vmem((2, *half_block), F32),
        vmem(block, F32),
        vmem(block, BF),
        vmem((2, lanes, panel_rows), BF),
        vmem((2, *turned), F32),
        vmem((2, *turned), F32),
        vmem((2, rows_n, *turned), BF),
        vmem((2, rows_n, *turned), BF),
        vmem((2, width + 8, width), F32),
        vmem((width + 8, width), F32),
        vmem((rows_n, *grads), F32),
        vmem((rows_n, *grads), F32),
        vmem(grads, F32),
        vmem((chips, 3, tile_rows, lanes), F32),
        vmem((chips, 3, tile_rows, lanes), F32),
        vmem((rows_n, tile_rows, lanes), F32),
        vmem((2, chips, rows_n, tile_rows, lanes), F32),
        dma((BUFFERS,)),
        dma((9,)),
        dma((2, rows_n)),
        dma((2, rows_n)),
    ]
    scratch += [dma((2, chips))] * 8 + [dma((2, rows_n))] * 2 + [dma((1,))] * 2 + [dma((rows_n,))] * 2
    scratch += [dma((chips,))] * 2 + [dma((rows_n,))] * 2 + [dma((chips,))] * 4
    results = pl.pallas_call(
        functools.partial(kernel, rows_n, reps_n, scale),
        out_shape=(
            vmem(block, BF),
            vmem(block, BF),
            vmem((width, width), F32),
            vmem((width, width), F32),
            vmem((1, width), F32),
        ),
        in_specs=[anywhere] * 9,
        out_specs=(pl.BlockSpec(memory_space=vmem),) * 5,
        scratch_shapes=scratch,
        compiler_params=pltpu.CompilerParams(
            collective_id=0, has_side_effects=True, vmem_limit_bytes=56 * 1024 * 1024
        ),
        name="layer",
    )(
        features,
        self_weight,
        neigh_weight,
        out_bias.reshape(1, width),
        tile_masks.reshape(panel_rows * slots, tile),
        tile_live.T,
        tile_columns.T,
        node_degree.reshape(1, share),
        cotangent,
    )
    hidden, grad_features, grad_self, grad_neigh, grad_bias = pl.pallas_call(
        store,
        out_shape=tuple(jax.ShapeDtypeStruct(one.shape, one.dtype) for one in results),
        in_specs=[pl.BlockSpec(memory_space=vmem)] * 5,
        out_specs=(anywhere,) * 5,
        scratch_shapes=[dma((5,))],
        name="store",
    )(*[pltpu.with_memory_space_constraint(one, vmem) for one in results])
    return (hidden, grad_features, grad_self, grad_neigh, grad_bias.reshape(width))


def solution(mesh):
    return jax.shard_map(
        per_device,
        mesh=mesh,
        in_specs=(
            P("row", None),
            P(),
            P(),
            P(),
            P("row", "rep", None),
            P("row", "rep"),
            P("row", "rep"),
            P(("row", "rep")),
            P(("row", "rep"), None),
        ),
        out_specs=(P(("row", "rep"), None), P(("row", "rep"), None), P(), P(), P()),
        check_vma=False,
    )
```
